32 devices in a mesh: row: 4 (over z), col: 8 (over y, x, core).
Axes of the slice: x: 2, y: 2, z: 4, core: 2. Of those that a mesh axis runs over, the one named last changes fastest.
Arguments:
- features: bfloat16 [12288, 128], P(('row', 'col')), may hold values from -6 to 6
- weight: bfloat16 [128, 128], replicated, may hold values from -0.5 to 0.5
- tiles: bfloat16 [4, 2048, 128, 128], P('row', 'col'), may hold values from -0.09375 to 0.09375
- tile_dest: int32 [4, 2048], P('row', 'col'), may hold values from 0 to 23, as said below
- tile_src: int32 [4, 2048], P('row', 'col'), may hold values from 0 to 11, as said below
- tile_count: int32 [4, 8], P('row', 'col'), may hold values from 32 to 256, as said below
- source_of: int32 [12288], P(('row', 'col')), may hold values from 0 to 12287, as said below
- out_grad: bfloat16 [12288, 128], P(('row', 'col')), may hold values from -6 to 6
Outputs:
- activations: bfloat16 [12288, 128], P(('row', 'col'))
- feature_grad: bfloat16 [12288, 128], P(('row', 'col'))
- weight_grad: float32 [128, 128], replicated
The draws below stay inside these ranges and needn't reach their ends.
Inputs may be any that keep to these rules, and one draw needn't show every extreme that they name: `tile_dest`: the slots of one device name distinct tiles. `tile_src`: the slots of one device name distinct tiles. `tile_count`: some device has all of its 256 slots live. `source_of`: a permutation of the 12288 vertices; of the 384 destination positions of each device, exactly 12 hold source vertices of each device.
All inputs are finite; a program needn't handle non-finite values.
Results may differ from the reference program's by a relative error of at most 0.017.
Values may be sent and summed in bfloat16 or wider, within the bound.
No kernel may reach another device: no remote copies, remote signals or barrier semaphores. Data moves between devices by JAX's collectives and lax.ppermute only.
A program may use at most 64 MiB of HBM per device.

```python
import math
import jax
import jax.numpy as jnp
from jax import lax

WIDTH = 128
TILE = 128
ROWS_DEV = 384
TILES_DEV = 256
STRIPS = 4
COLUMNS = 8
GROUPS = 32
NODES = 12288
PAIR = 12
STRIP_BLOCKS = 24
GROUP_BLOCKS = 12
SLOTS = 2048
N_COL = 8


def tile_layout(key):
    key_cells = jax.random.fold_in(key, 11)
    grid_size = STRIP_BLOCKS * GROUP_BLOCKS
    key_list = jax.random.split(key_cells, GROUPS)
    chosen = jax.vmap(lambda subkey: jax.random.permutation(subkey, grid_size)[:TILES_DEV])(key_list)
    return chosen.reshape(STRIPS, SLOTS).astype(jnp.int32)


def draw_tile_dest(key, part):
    return (tile_layout(key) // GROUP_BLOCKS).astype(jnp.int32)


def draw_tile_src(key, part):
    return (tile_layout(key) % GROUP_BLOCKS).astype(jnp.int32)


def draw_tile_count(key, part):
    key_load = jax.random.fold_in(key, 12)
    raw_load = jax.random.randint(key_load, (GROUPS,), 0, TILES_DEV + 1)
    loads = jnp.maximum(TILES_DEV // 8, raw_load * raw_load // TILES_DEV)
    full_device = jax.random.randint(jax.random.fold_in(key_load, 1), (), 0, GROUPS)
    loads = jnp.where(jnp.arange(GROUPS) == full_device, TILES_DEV, loads)
    return loads.reshape(STRIPS, COLUMNS).astype(jnp.int32)


def draw_source_of(key, part):
    key_send = jax.random.fold_in(key, 21)
    key_place = jax.random.fold_in(key, 22)
    local_perm = jax.vmap(lambda subkey: jax.random.permutation(subkey, ROWS_DEV))(jax.random.split(key_send, GROUPS))
    vertex = local_perm + jnp.arange(GROUPS)[:, None] * ROWS_DEV
    vertex = vertex.reshape(GROUPS, GROUPS, PAIR).transpose(1, 0, 2).reshape(GROUPS, ROWS_DEV)
    shuffle = jax.vmap(lambda subkey: jax.random.permutation(subkey, ROWS_DEV))(jax.random.split(key_place, GROUPS))
    placed = jnp.take_along_axis(vertex, shuffle, axis=1)
    return placed.reshape(NODES).astype(jnp.int32)


def block_scale(rng, shape, shards, least, high):
    loudness = 1.0
    for axis_at, blocks in shards:
        draws = jax.random.uniform(jax.random.fold_in(jax.random.fold_in(rng, 6), axis_at), (blocks,), jnp.float32, least / len(shards), high / len(shards))
        loudness = loudness * jnp.repeat(jnp.exp(draws), shape[axis_at] // blocks).reshape((-1,) + (1,) * (len(shape) - 1 - axis_at))
    return loudness


def scatter_about(own_key, extent, scale, reach, shards=(), kind=jnp.bfloat16):
    drawn = scale * jax.random.normal(own_key, extent, jnp.float32)
    if shards:
        drawn = drawn * block_scale(own_key, extent, shards, -0.22, 0.18)
    return jnp.clip(drawn, -reach, reach).astype(kind)


def setup_inputs(seed: int = 0) -> dict:
    key_of = jax.random.split(jax.random.key(seed), 9)
    features = scatter_about(key_of[0], (NODES, WIDTH), 1.0, 6.0, ((0, 32),))
    weight = scatter_about(key_of[1], (WIDTH, WIDTH), WIDTH ** -0.5, 0.5)
    tiles = scatter_about(key_of[2], (STRIPS, SLOTS, TILE, TILE), (max(TILE, TILE * TILES_DEV * N_COL // (3 * STRIP_BLOCKS))) ** -0.5, 0.09375, ((0, 4), (1, 8)))
    tile_dest = draw_tile_dest(jax.random.fold_in(key_of[8], 71), 0)
    tile_src = draw_tile_src(jax.random.fold_in(key_of[8], 71), 0)
    tile_count = draw_tile_count(jax.random.fold_in(key_of[8], 71), 0)
    source_of = draw_source_of(jax.random.fold_in(key_of[8], 71), 0)
    out_grad = scatter_about(key_of[7], (NODES, WIDTH), 1.0, 6.0, ((0, 32),))
    return dict(features=features, weight=weight, tiles=tiles, tile_dest=tile_dest, tile_src=tile_src, tile_count=tile_count, source_of=source_of, out_grad=out_grad)


def silu_slope(values):
    sigma = jax.nn.sigmoid(values)
    return sigma * (1.0 + values * (1.0 - sigma))

def reference(features, weight, tiles, tile_dest, tile_src, tile_count, source_of, out_grad):
    hidden = jnp.dot(features, weight, preferred_element_type=jnp.float32).astype(jnp.bfloat16)
    group_rows = hidden.reshape(STRIPS, COLUMNS, ROWS_DEV, WIDTH).transpose(1, 0, 2, 3)
    group_rows = group_rows.reshape(COLUMNS, GROUP_BLOCKS, TILE, WIDTH)
    tile_sets = tiles.reshape(GROUPS, TILES_DEV, TILE, TILE)
    dest_sets = tile_dest.reshape(GROUPS, TILES_DEV)
    source_sets = tile_src.reshape(GROUPS, TILES_DEV)
    load_sets = tile_count.reshape(GROUPS)
    devices = jnp.arange(GROUPS, dtype=jnp.int32)

    def forward_step(totals, device):
        strip_idx = device // COLUMNS
        col_idx = device % COLUMNS
        operand = group_rows[col_idx][source_sets[device]]
        product = jnp.einsum('bij,bjf->bif', tile_sets[device].astype(jnp.float32), operand.astype(jnp.float32))
        live_mask = jnp.arange(TILES_DEV) < load_sets[device]
        product = jnp.where(live_mask[:, None, None], product, 0.0)
        return (totals.at[strip_idx, dest_sets[device]].add(product), None)
    start_sums = jnp.zeros((STRIPS, STRIP_BLOCKS, TILE, WIDTH), jnp.float32)
    strip_sums, _ = lax.scan(forward_step, start_sums, devices)
    pre = strip_sums.reshape(NODES, WIDTH).astype(jnp.bfloat16)
    pre_float = pre.astype(jnp.float32)
    act_dest = jax.nn.silu(pre_float).astype(jnp.bfloat16)
    activations = jnp.zeros((NODES, WIDTH), jnp.bfloat16).at[source_of].set(act_dest)
    dest_grad = out_grad[source_of].astype(jnp.float32)
    pre_grad = (dest_grad * silu_slope(pre_float)).astype(jnp.bfloat16)
    strip_grad = pre_grad.reshape(STRIPS, STRIP_BLOCKS, TILE, WIDTH)

    def backward_step(totals, device):
        strip_idx = device // COLUMNS
        col_idx = device % COLUMNS
        operand = strip_grad[strip_idx][dest_sets[device]]
        product = jnp.einsum('bji,bjf->bif', tile_sets[device].astype(jnp.float32), operand.astype(jnp.float32))
        live_mask = jnp.arange(TILES_DEV) < load_sets[device]
        product = jnp.where(live_mask[:, None, None], product, 0.0)
        return (totals.at[col_idx, source_sets[device]].add(product), None)
    start_grads = jnp.zeros((COLUMNS, GROUP_BLOCKS, TILE, WIDTH), jnp.float32)
    group_grads, _ = lax.scan(backward_step, start_grads, devices)
    hidden_grad = group_grads.reshape(COLUMNS, STRIPS, ROWS_DEV, WIDTH).transpose(1, 0, 2, 3)
    hidden_grad = hidden_grad.reshape(NODES, WIDTH).astype(jnp.bfloat16)
    feature_grad = jnp.dot(hidden_grad, weight.T, preferred_element_type=jnp.float32).astype(jnp.bfloat16)
    weight_grad = jnp.dot(features.T, hidden_grad, preferred_element_type=jnp.float32) / math.sqrt(NODES)
    return (activations, feature_grad, weight_grad)
```

```python
import functools
import math

import jax
import jax.numpy as jnp
from jax import lax
from jax.experimental import pallas as pl
from jax.experimental.pallas import tpu as pltpu
from jax.sharding import PartitionSpec as P


BF16 = jnp.bfloat16
F32 = jnp.float32


def xor_pairs(size, bit):
    return [(i, i ^ bit) for i in range(size)]


def build_kernel(count_ref, row_ref, col_ref, tiles_ref, dense_ref, sem):
    edge = tiles_ref.shape[-1]
    rows = dense_ref.shape[0]
    chunk = 2 * edge

    def clear(step, carry):
        dense_ref[pl.ds(pl.multiple_of(step * chunk, chunk), chunk), :] = jnp.zeros(
            (chunk, dense_ref.shape[1]), dense_ref.dtype
        )
        return carry

    lax.fori_loop(0, rows // chunk, clear, 0)
    live = count_ref[0]

    def copy(slot):
        row = pl.multiple_of(row_ref[slot] * edge, edge)
        col = pl.multiple_of(col_ref[slot] * edge, edge)
        return pltpu.make_async_copy(
            tiles_ref.at[slot], dense_ref.at[pl.ds(row, edge), pl.ds(col, edge)], sem
        )

    def start(slot, carry):
        copy(slot).start()
        return carry

    def wait(slot, carry):
        copy(slot).wait()
        return carry

    lax.fori_loop(0, live, start, 0)
    lax.fori_loop(0, live, wait, 0)


def build_dense(tile_set, row_block, col_block, live_count, rows, cols):
    return pl.pallas_call(
        build_kernel,
        out_shape=jax.ShapeDtypeStruct((rows, cols), BF16),
        in_specs=[
            pl.BlockSpec(memory_space=pltpu.SMEM),
            pl.BlockSpec(memory_space=pltpu.SMEM),
            pl.BlockSpec(memory_space=pltpu.SMEM),
            pl.BlockSpec(memory_space=pl.ANY),
        ],
        out_specs=pl.BlockSpec(memory_space=pltpu.VMEM),
        scratch_shapes=[pltpu.SemaphoreType.DMA],
        compiler_params=pltpu.CompilerParams(
            vmem_limit_bytes=rows * cols * 2 + (1 << 20),
        ),
        cost_estimate=pl.CostEstimate(flops=0, bytes_accessed=tile_set.size * 2, transcendentals=0),
        name="build_dense",
    )(live_count, row_block, col_block, tile_set)


def local(features, weight, tiles, tile_dest, tile_src, tile_count, source_of, out_grad):
    rows, width = features.shape
    edge = tiles.shape[-1]
    n_row = lax.axis_size("row")
    n_col = lax.axis_size("col")
    n_all = n_row * n_col
    pair = rows // n_all
    per = rows // edge
    my_row = lax.axis_index("row")
    my_col = lax.axis_index("col")

    def row_swap(value, bit):
        return lax.ppermute(value, "row", xor_pairs(n_row, bit))

    def col_swap(value, bit):
        return lax.ppermute(value, "col", xor_pairs(n_col, bit))

    def dot(a, b, dims=((1,), (0,))):
        return lax.dot_general(a, b, (dims, ((), ())), preferred_element_type=F32)

    feat = jnp.concatenate([features] + [row_swap(features, k) for k in range(1, n_row)], axis=0)

    row_block = (tile_dest[0] // per ^ my_col) * per + tile_dest[0] % per
    col_block = (tile_src[0] // per ^ my_row) * per + tile_src[0] % per
    dense = build_dense(
        tiles[0], row_block, col_block, tile_count[0], n_col * rows, n_row * rows
    )

    owner = source_of // rows
    place = source_of % rows
    is_owner = owner[:, None] == jnp.arange(n_all)[None, :]
    index = jnp.arange(rows)
    before = (index[:, None] > index[None, :]).astype(BF16)
    earlier = dot(before, is_owner.astype(BF16))
    rank = jnp.sum(jnp.where(is_owner, earlier, 0.0), axis=1).astype(jnp.int32)
    slot = owner * pair + rank
    to_slot = slot[None, :] == index[:, None]
    send_ids = jnp.sum(jnp.where(to_slot, place[None, :], 0), axis=1)
    to_slot = to_slot.astype(BF16)

    def exchange(value):
        return lax.all_to_all(value, ("row", "col"), split_axis=0, concat_axis=0, tiled=True)

    got_ids = exchange(send_ids.reshape(n_all, pair)).reshape(rows)
    at_owner = (got_ids[:, None] == index[None, :]).astype(BF16)
    returned = exchange(dot(at_owner, out_grad).astype(BF16))
    dest_grad = dot(to_slot, returned, ((0,), (0,)))

    partial_sum = dot(dense, feat).astype(BF16)
    mixed = partial_sum[:rows].astype(F32)
    for k in range(1, n_col):
        mixed = mixed + col_swap(partial_sum[k * rows : (k + 1) * rows], k).astype(F32)
    mixed = mixed.astype(BF16)
    pre = dot(mixed, weight).astype(BF16).astype(F32)
    sigma = jax.nn.sigmoid(pre)
    act = (pre * sigma).astype(BF16)
    grad = (dest_grad * (sigma * (1.0 + pre * (1.0 - sigma)))).astype(BF16)

    strip_grad = jnp.concatenate([grad] + [col_swap(grad, k) for k in range(1, n_col)], axis=0)

    got_act = exchange(dot(to_slot, act).astype(BF16))
    activations = dot(at_owner, got_act, ((0,), (0,))).astype(BF16)

    weight_sum = dot(mixed, grad, ((0,), (0,)))
    bit = 1
    while bit < n_col:
        sent = weight_sum.astype(BF16)
        weight_sum = sent.astype(F32) + col_swap(sent, bit).astype(F32)
        bit *= 2
    bit = 1
    while bit < n_row:
        sent = weight_sum.astype(BF16)
        weight_sum = sent.astype(F32) + row_swap(sent, bit).astype(F32)
        bit *= 2
    weight_grad = weight_sum * (1.0 / math.sqrt(rows * n_all))

    group_part = dot(dense, strip_grad, ((0,), (0,))).astype(BF16)
    hidden_grad = group_part[:rows].astype(F32)
    for k in range(1, n_row):
        hidden_grad = hidden_grad + row_swap(group_part[k * rows : (k + 1) * rows], k).astype(F32)
    hidden_grad = hidden_grad.astype(BF16)
    feature_grad = dot(hidden_grad, weight, ((1,), (1,))).astype(BF16)
    return (activations, feature_grad, weight_grad)


def solution(mesh):
    placed = (
        P(("row", "col"), None),
        P(),
        P("row", "col", None, None),
        P("row", "col"),
        P("row", "col"),
        P("row", "col"),
        P(("row", "col")),
        P(("row", "col"), None),
    )
    return jax.shard_map(
        local,
        mesh=mesh,
        in_specs=placed,
        out_specs=(P(("row", "col"), None), P(("row", "col"), None), P()),
        check_vma=False,
    )
```

```python
import functools
import math

import jax
import jax.numpy as jnp
from jax import lax
from jax.experimental import pallas as pl
from jax.experimental.pallas import tpu as pltpu
from jax.sharding import PartitionSpec as P


BF16 = jnp.bfloat16
F32 = jnp.float32
I32 = jnp.int32
LANES = 128
GRANT = 16 << 20
KEPT = 24 << 20


def xor_pairs(size, bit):
    return [(i, i ^ bit) for i in range(size)]


def dot(a, b, left=1, right=0):
    return lax.dot_general(a, b, (((left,), (right,)), ((), ())), preferred_element_type=F32)


def iota(shape, dim):
    return lax.broadcasted_iota(I32, shape, dim)


def call(body, out_shape, operands, spaces, scratch=(), name=None, flops=0, moved=0, grant=GRANT):
    single = not isinstance(out_shape, (list, tuple))
    spec = pl.BlockSpec(memory_space=pltpu.VMEM)
    return pl.pallas_call(
        body,
        out_shape=out_shape,
        in_specs=[pl.BlockSpec(memory_space=space) for space in spaces],
        out_specs=spec if single else [spec] * len(out_shape),
        scratch_shapes=list(scratch),
        compiler_params=pltpu.CompilerParams(vmem_limit_bytes=grant),
        cost_estimate=pl.CostEstimate(flops=flops, bytes_accessed=moved, transcendentals=0),
        name=name,
    )(*operands)


def build_body(per, dest_ref, src_ref, count_ref, tiles_ref, dense_ref, sem):
    edge = tiles_ref.shape[-1]
    rows, cols = dense_ref.shape
    chunk = 2 * edge
    my_row = lax.axis_index("row")
    my_col = lax.axis_index("col")

    def clear(step, carry):
        at = pl.multiple_of(step * chunk, chunk)
        dense_ref[pl.ds(at, chunk), :] = jnp.zeros((chunk, cols), BF16)
        return carry

    lax.fori_loop(0, rows // chunk, clear, 0)
    live = count_ref[0, 0]

    def start(slot, carry):
        dest = dest_ref[0, slot]
        src = src_ref[0, slot]
        dest_part = lax.div(dest, per)
        src_part = lax.div(src, per)
        row = dest + ((dest_part ^ my_col) - dest_part) * per
        col = src + ((src_part ^ my_row) - src_part) * per
        pltpu.make_async_copy(
            tiles_ref.at[slot],
            dense_ref.at[
                pl.ds(pl.multiple_of(row * edge, edge), edge),
                pl.ds(pl.multiple_of(col * edge, edge), edge),
            ],
            sem,
        ).start()
        return carry

    def wait(slot, carry):
        pltpu.make_async_copy(
            tiles_ref.at[0], dense_ref.at[pl.ds(0, edge), pl.ds(0, edge)], sem
        ).wait()
        return carry

    lax.fori_loop(0, live, start, 0)
    lax.fori_loop(0, live, wait, 0)


def slot_body(n_row, n_col, per_pair, source_ref, table_ref, slot_ref):
    rows = source_ref.shape[-1]
    slots = table_ref.shape[-1]
    my_row = lax.axis_index("row")
    my_col = lax.axis_index("col")
    source = source_ref[...]
    owner = ((source.astype(F32) + 0.5) * (1.0 / rows)).astype(I32)
    place = source - owner * rows + 1
    n_all = n_row * n_col
    mine = iota((n_all, rows), 0) == owner
    before = (iota((rows, rows), 0) < iota((rows, rows), 1)).astype(BF16)
    earlier = dot(mine.astype(BF16), before)
    rank = jnp.sum(jnp.where(mine, earlier, 0.0), axis=0, keepdims=True).astype(I32)
    shift = n_col.bit_length() - 1
    far_row = (owner >> shift) ^ my_row
    far_col = (owner & (n_col - 1)) ^ my_col
    by_row = (far_row * n_col + far_col) * per_pair + rank
    by_col = (far_col * n_row + far_row) * per_pair + rank
    hot = (iota((slots, rows), 0) == by_row).astype(BF16)
    high = jnp.broadcast_to((place >> 7).astype(F32), (8, rows)).astype(BF16)
    low = jnp.broadcast_to((place & 127).astype(F32), (8, rows)).astype(BF16)
    table_ref[...] = (dot(high, hot, 1, 1) * 128.0 + dot(low, hot, 1, 1)).astype(I32)
    slot_ref[...] = jnp.broadcast_to(by_col, (8, rows))


def forward_body(n_row, n_col, per_pair, *refs):
    dense_ref, table_ref = refs[:2]
    got = refs[2 : 2 + n_row]
    out = refs[2 + n_row :]
    rows = got[0].shape[0] // 2
    lanes = n_col * per_pair
    feat = jnp.concatenate([ref[:rows, :] for ref in got], axis=0)
    for k in range(n_col):
        out[k][:rows, :] = dot(dense_ref[k * rows : (k + 1) * rows, :], feat).astype(BF16)
    for r in range(n_row):
        place = table_ref[0:1, r * lanes : (r + 1) * lanes]
        hot = (iota((rows, lanes), 0) + 1 == place).astype(BF16)
        picked = dot(hot, got[r][rows:, :], 0, 0).astype(BF16)
        for k in range(n_col):
            at = rows + r * per_pair
            out[k][at : at + per_pair, :] = picked[k * per_pair : (k + 1) * per_pair, :]


def middle_body(n_row, n_col, per_pair, *refs):
    slot_ref, weight_ref = refs[:2]
    got = refs[2 : 2 + n_col]
    out = refs[2 + n_col : 2 + 2 * n_col]
    term_ref = refs[-1]
    tail = n_row * per_pair
    rows = got[0].shape[0] - tail
    slots = n_col * tail
    mixed = got[0][:rows, :].astype(F32)
    for k in range(1, n_col):
        mixed = mixed + got[k][:rows, :].astype(F32)
    mixed = mixed.astype(BF16)
    pre = dot(mixed, weight_ref[...]).astype(BF16).astype(F32)
    sigma = jax.nn.sigmoid(pre)
    act = (pre * sigma).astype(BF16)
    hot = (iota((slots, rows), 0) == slot_ref[0:1, :]).astype(BF16)
    cotangent = jnp.concatenate([ref[rows:, :] for ref in got], axis=0)
    dest_grad = dot(hot, cotangent, 0, 0)
    grad = (dest_grad * (sigma * (1.0 + pre * (1.0 - sigma)))).astype(BF16)
    sent = dot(hot, act).astype(BF16)
    for k in range(n_col):
        out[k][:rows, :] = grad
        out[k][rows:, :] = sent[k * tail : (k + 1) * tail, :]
    term_ref[...] = dot(mixed, grad, 0, 0).astype(BF16)


def backward_body(n_row, n_col, per_pair, *refs):
    dense_ref, table_ref = refs[:2]
    got = refs[2 : 2 + n_col]
    out = refs[2 + n_col :]
    rows = got[0].shape[0] - n_row * per_pair
    lanes = n_col * per_pair
    grad = jnp.concatenate([ref[:rows, :].T for ref in got], axis=1)
    total = n_row * rows
    width = 2 * LANES
    for at in range(0, total, width):
        size = min(width, total - at)
        part = dot(grad, dense_ref[:, at : at + size]).T.astype(BF16)
        for half in range(0, size, LANES):
            r, row = divmod(at + half, rows)
            out[r][row : row + LANES, :] = part[half : half + LANES, :]
    for r in range(n_row):
        for k in range(n_col):
            at = rows + k * per_pair
            tail = rows + r * per_pair
            out[r][at : at + per_pair, :] = got[k][tail : tail + per_pair, :]
        base = rows + lanes
        marks = out[r].shape[0] - base
        row = iota((marks, LANES), 0)
        block = jnp.zeros((marks, LANES), F32)
        for piece in range(lanes // LANES):
            at = r * lanes + piece * LANES
            place = table_ref[0:1, at : at + LANES]
            block = jnp.where(row == 2 * piece, (place >> 7).astype(F32), block)
            block = jnp.where(row == 2 * piece + 1, (place & 127).astype(F32), block)
        out[r][base:, :] = block.astype(BF16)


def final_body(n_row, n_col, per_pair, *refs):
    weight_ref = refs[0]
    got = refs[1 : 1 + n_row]
    act_ref, grad_ref = refs[1 + n_row :]
    rows = act_ref.shape[0]
    lanes = n_col * per_pair
    hidden = got[0][:rows, :].astype(F32)
    for r in range(1, n_row):
        hidden = hidden + got[r][:rows, :].astype(F32)
    grad_ref[...] = dot(hidden.astype(BF16), weight_ref[...], 1, 1).astype(BF16)
    act = jnp.zeros(act_ref.shape, F32)
    index = iota((rows, LANES), 0) + 1
    for r in range(n_row):
        marks = got[r][rows + lanes :, :].astype(F32)
        for piece in range(lanes // LANES):
            high = marks[2 * piece : 2 * piece + 1, :]
            low = marks[2 * piece + 1 : 2 * piece + 2, :]
            place = (high * 128.0 + low).astype(I32)
            at = rows + piece * LANES
            act = act + dot((index == place).astype(BF16), got[r][at : at + LANES, :])
    act_ref[...] = act.astype(BF16)


def local(features, weight, tiles, tile_dest, tile_src, tile_count, source_of, out_grad):
    rows, width = features.shape
    edge = tiles.shape[-1]
    n_row = lax.axis_size("row")
    n_col = lax.axis_size("col")
    n_all = n_row * n_col
    per_pair = -(-(rows // n_all) // 16) * 16
    slots = n_all * per_pair
    lanes = n_col * per_pair
    tail = n_row * per_pair
    marks = -(-2 * (lanes // LANES) // 16) * 16
    sizes = (n_row, n_col, per_pair)

    def row_swap(value, bit):
        return lax.ppermute(value, "row", xor_pairs(n_row, bit))

    def col_swap(value, bit):
        return lax.ppermute(value, "col", xor_pairs(n_col, bit))

    def block(count, kind=BF16):
        return jax.ShapeDtypeStruct((count, width), kind)

    vmem = pltpu.VMEM
    smem = pltpu.SMEM

    given = jnp.concatenate([features, out_grad], axis=0)
    group = [given] + [row_swap(given, k) for k in range(1, n_row)]

    table, slot = call(
        functools.partial(slot_body, *sizes),
        [jax.ShapeDtypeStruct((8, slots), I32), jax.ShapeDtypeStruct((8, rows), I32)],
        (source_of.reshape(1, rows),),
        (vmem,),
        name="slots",
        moved=8 * slots * 4,
    )
    far_col = jnp.arange(slots)[None, :] // per_pair % n_col
    bit = 1
    while bit < n_col:
        table = jnp.where(far_col & bit != 0, col_swap(table, bit), table)
        bit *= 2

    dense_bytes = 2 * n_all * rows * rows
    kept = dense_bytes <= KEPT
    dense_shape = (n_col * rows, n_row * rows)
    grant = GRANT if kept else dense_bytes + GRANT
    dense = call(
        functools.partial(build_body, rows // edge),
        pltpu.VMEM(dense_shape, BF16) if kept else jax.ShapeDtypeStruct(dense_shape, BF16),
        (
            tile_dest,
            tile_src,
            tile_count,
            pltpu.with_memory_space_constraint(tiles.reshape(tiles.shape[1:]), pltpu.HBM),
        ),
        (smem, smem, smem, pltpu.HBM),
        scratch=[pltpu.SemaphoreType.DMA],
        name="build",
        grant=grant,
        moved=tiles.size * 2,
    )

    work = 2 * n_all * rows * rows * width
    partial_sum = call(
        functools.partial(forward_body, *sizes),
        [block(rows + tail)] * n_col,
        (dense, table, *group),
        (vmem,) * (2 + n_row),
        name="forward",
        grant=grant,
        flops=work,
    )
    partial_sum = [partial_sum[0]] + [col_swap(partial_sum[k], k) for k in range(1, n_col)]

    *sent, term = call(
        functools.partial(middle_body, *sizes),
        [block(rows + tail)] * n_col + [block(width)],
        (slot, weight, *partial_sum),
        (vmem,) * (2 + n_col),
        name="middle",
        flops=8 * slots * rows * width,
    )
    strip = [sent[0]] + [col_swap(sent[k], k) for k in range(1, n_col)]

    for swap, size in ((row_swap, n_row), (col_swap, n_col)):
        bit = 1
        while bit < size:
            total = term.astype(F32) + swap(term, bit).astype(F32)
            term = total.astype(BF16)
            bit *= 2
    weight_grad = total * (1.0 / math.sqrt(rows * n_all))

    part = call(
        functools.partial(backward_body, *sizes),
        [block(rows + lanes + marks)] * n_row,
        (dense, table, *strip),
        (vmem,) * (2 + n_col),
        name="backward",
        grant=grant,
        flops=work,
    )
    part = [part[0]] + [row_swap(part[k], k) for k in range(1, n_row)]
    activations, feature_grad = call(
        functools.partial(final_body, *sizes),
        [block(rows), block(rows)],
        (weight, *part),
        (vmem,) * (1 + n_row),
        name="final",
        flops=8 * slots * rows * width,
    )
    return (activations, feature_grad, weight_grad)


def solution(mesh):
    placed = (
        P(("row", "col"), None),
        P(),
        P("row", "col", None, None),
        P("row", "col"),
        P("row", "col"),
        P("row", "col"),
        P(("row", "col")),
        P(("row", "col"), None),
    )
    return jax.shard_map(
        local,
        mesh=mesh,
        in_specs=placed,
        out_specs=(P(("row", "col"), None), P(("row", "col"), None), P()),
        check_vma=False,
    )
```

```python
import functools
import math

import jax
import jax.numpy as jnp
from jax import lax
from jax.experimental import pallas as pl
from jax.experimental.pallas import tpu as pltpu
from jax.sharding import PartitionSpec as P


BF16 = jnp.bfloat16
F32 = jnp.float32
I32 = jnp.int32
LANES = 128
GRANT = 16 << 20
KEPT = 24 << 20


def xor_pairs(size, bit):
    return [(i, i ^ bit) for i in range(size)]


def dot(a, b, left=1, right=0):
    return lax.dot_general(a, b, (((left,), (right,)), ((), ())), preferred_element_type=F32)


def iota(shape, dim):
    return lax.broadcasted_iota(I32, shape, dim)


def call(body, out_shape, operands, spaces, scratch=(), flops=0, moved=0, grant=GRANT):
    single = not isinstance(out_shape, (list, tuple))
    spec = pl.BlockSpec(memory_space=pltpu.VMEM)
    return pl.pallas_call(
        body,
        out_shape=out_shape,
        in_specs=[pl.BlockSpec(memory_space=space) for space in spaces],
        out_specs=spec if single else [spec] * len(out_shape),
        scratch_shapes=list(scratch),
        compiler_params=pltpu.CompilerParams(vmem_limit_bytes=grant),
        cost_estimate=pl.CostEstimate(flops=flops, bytes_accessed=moved, transcendentals=0),
    )(*operands)


def half_place(part, me, chips):
    far = part ^ me
    return (1 - (far & 1)) * chips + (far >> 1)


def build_body(
    sizes,
    dest_hbm,
    src_hbm,
    count_ref,
    source_hbm,
    feat_hbm,
    cot_hbm,
    tiles_ref,
    dense_ref,
    table_ref,
    slot_ref,
    feat_ref,
    cot_ref,
    dest_ref,
    src_ref,
    source_ref,
    row_ref,
    col_ref,
    sem,
    near,
):
    n_row, n_col, span = sizes
    edge = tiles_ref.shape[-1]
    rows, cols = dense_ref.shape
    per = cols // (n_row * edge)
    chunk = 2 * edge
    my_row = lax.axis_index("row")
    my_col = lax.axis_index("col")
    loads = [
        pltpu.make_async_copy(dest_hbm, dest_ref, near.at[0]),
        pltpu.make_async_copy(src_hbm, src_ref, near.at[1]),
        pltpu.make_async_copy(source_hbm, source_ref, near.at[2]),
    ]
    rows_in = [
        pltpu.make_async_copy(feat_hbm, feat_ref, near.at[3]),
        pltpu.make_async_copy(cot_hbm, cot_ref, near.at[4]),
    ]
    for load in loads + rows_in:
        load.start()
    for part in range(n_col):
        for block in range(per):
            row_ref[part * per + block] = (half_place(part, my_col, n_col // 2) * per + block) * edge
    for part in range(n_row):
        for block in range(per):
            col_ref[part * per + block] = ((part ^ my_row) * per + block) * edge

    def clear(step, carry):
        at = pl.multiple_of(step * chunk, chunk)
        dense_ref[pl.ds(at, chunk), :] = jnp.zeros((chunk, cols), BF16)
        return carry

    lax.fori_loop(0, rows // chunk, clear, 0)
    for load in loads:
        load.wait()
    live = count_ref[0, 0]

    def start(slot):
        row = pl.multiple_of(row_ref[dest_ref[0, slot]], edge)
        col = pl.multiple_of(col_ref[src_ref[0, slot]], edge)
        pltpu.make_async_copy(
            tiles_ref.at[slot], dense_ref.at[pl.ds(row, edge), pl.ds(col, edge)], sem
        ).start()

    def start_some(step, carry):
        for at in range(4):
            start(step * 4 + at)
        return carry

    def start_one(slot, carry):
        start(slot)
        return carry

    some = live >> 2
    lax.fori_loop(0, some, start_some, 0)
    lax.fori_loop(some * 4, live, start_one, 0)

    slot_work(n_row, n_col, span, source_ref, table_ref, slot_ref)
    for load in rows_in:
        load.wait()

    def arrived(count):
        part = dense_ref.at[pl.ds(0, edge), pl.ds(0, count * edge)]
        return pltpu.make_async_copy(part, part, sem)

    def wait_many(step, carry):
        arrived(8).wait()
        return carry

    def wait_one(step, carry):
        arrived(1).wait()
        return carry

    lax.fori_loop(0, live >> 3, wait_many, 0)
    lax.fori_loop(0, live & 7, wait_one, 0)


def slot_work(n_row, n_col, span, source_ref, table_ref, slot_ref):
    rows = source_ref.shape[-1]
    slots = table_ref.shape[-1]
    n_all = n_row * n_col
    my_row = lax.axis_index("row")
    my_col = lax.axis_index("col")
    source = source_ref[...].reshape(1, rows)
    owner = ((source.astype(F32) + 0.5) * (1.0 / rows)).astype(I32)
    place = source - owner * rows + 1
    mine = iota((n_all, rows), 0) == owner
    before = (iota((rows, rows), 0) < iota((rows, rows), 1)).astype(BF16)
    earlier = dot(mine.astype(BF16), before)
    rank = jnp.sum(jnp.where(mine, earlier, 0.0), axis=0, keepdims=True).astype(I32)
    shift = n_col.bit_length() - 1
    far_row = (owner >> shift) ^ my_row
    far_col = (owner & (n_col - 1)) ^ my_col
    by_row = (far_row * n_col + far_col) * span + rank
    by_col = (far_col * n_row + far_row) * span + rank
    hot = (iota((slots, rows), 0) == by_row).astype(BF16)
    high = jnp.broadcast_to((place >> 7).astype(F32), (8, rows)).astype(BF16)
    low = jnp.broadcast_to((place & 127).astype(F32), (8, rows)).astype(BF16)
    table_ref[...] = (dot(high, hot, 1, 1) * 128.0 + dot(low, hot, 1, 1)).astype(I32)
    slot_ref[...] = jnp.where(iota((8, rows), 0) == 0, by_row, by_col)


def pick_body(n_row, n_col, span, table_ref, *refs):
    og = refs[:n_row]
    sides = refs[n_row:]
    rows = og[0].shape[0]
    lanes = n_col * span
    for r in range(n_row):
        place = table_ref[0:1, r * lanes : (r + 1) * lanes]
        hot = (iota((rows, lanes), 0) + 1 == place).astype(BF16)
        picked = dot(hot, og[r][...], 0, 0).astype(BF16)
        for k in range(n_col):
            at = ((k >> 1) * n_row + r) * span
            sides[k & 1][at : at + span, :] = picked[k * span : (k + 1) * span, :]


def pair_body(near_ref, far_ref, *out):
    size = out[0].shape[0] // 2
    for q, ref in enumerate(out):
        ref[:size, :] = near_ref[q * size : (q + 1) * size, :]
        ref[size:, :] = far_ref[q * size : (q + 1) * size, :]


def tree_sum(terms):
    terms = [term.astype(F32) for term in terms]
    while len(terms) > 1:
        terms = [terms[at] + terms[at + 1] for at in range(0, len(terms), 2)]
    return terms[0]


def forward_body(first, dense_ref, *refs):
    out = refs[-1]
    feat = jnp.concatenate([ref[...] for ref in refs[:-1]], axis=0)
    count = out.shape[0]
    step = 512 if count % 512 == 0 else 128
    for at in range(0, count, step):
        out[at : at + step, :] = dot(dense_ref[first + at : first + at + step, :], feat).astype(BF16)


def combine_body(own_ref, got_ref, *out):
    rows = out[0].shape[0]
    for at, ref in enumerate(out):
        part = slice(at * rows, (at + 1) * rows)
        ref[...] = (own_ref[part, :].astype(F32) + got_ref[part, :].astype(F32)).astype(BF16)


def middle_body(n_row, chips, slot_ref, table_ref, weight_ref, *refs):
    got = refs[:chips]
    back = refs[chips : 2 * chips]
    grad_ref = refs[2 * chips]
    out = refs[2 * chips + 1 :]
    rows, width = grad_ref.shape
    slots = table_ref.shape[1]
    lanes = slots // n_row
    marks = out[0].shape[0] - lanes - width
    mixed = got[0][...].astype(F32)
    for ref in got[1:]:
        mixed = mixed + ref[...].astype(F32)
    mixed = mixed.astype(BF16)
    pre = dot(mixed, weight_ref[...]).astype(BF16).astype(F32)
    sigma = jax.nn.sigmoid(pre)
    act = (pre * sigma).astype(BF16)
    returned = jnp.concatenate([ref[...] for ref in back], axis=0)
    hot = (iota((slots, rows), 0) == slot_ref[1:2, :]).astype(BF16)
    dest_grad = dot(hot, returned, 0, 0)
    grad = (dest_grad * (sigma * (1.0 + pre * (1.0 - sigma)))).astype(BF16)
    grad_ref[...] = grad
    hot = (iota((slots, rows), 0) == slot_ref[0:1, :]).astype(BF16)
    sent = dot(hot, act).astype(BF16)
    term = dot(mixed, grad, 0, 0).astype(BF16)
    row = iota((marks, LANES), 0)
    for r in range(n_row):
        out[r][:lanes, :] = sent[r * lanes : (r + 1) * lanes, :]
        block = jnp.zeros((marks, LANES), F32)
        for piece in range(lanes // LANES):
            at = r * lanes + piece * LANES
            place = table_ref[0:1, at : at + LANES]
            block = jnp.where(row == 2 * piece, (place >> 7).astype(F32), block)
            block = jnp.where(row == 2 * piece + 1, (place & 127).astype(F32), block)
        out[r][lanes : lanes + marks, :] = block.astype(BF16)
        out[r][lanes + marks :, :] = term


def side_body(n_row, n_col, span, *refs):
    got = refs[:n_row]
    sides = refs[n_row:]
    lanes = n_col * span
    width = got[0].shape[1]
    marks = got[0].shape[0] - lanes - width
    base = lanes * n_row // 2
    for r in range(n_row):
        for k in range(n_col):
            at = ((k >> 1) * n_row + r) * span
            sides[k & 1][at : at + span, :] = got[r][k * span : (k + 1) * span, :]
        for ref in sides:
            at = base + r * marks
            ref[at : at + marks, :] = got[r][lanes : lanes + marks, :]
    term = tree_sum([ref[lanes + marks :, :] for ref in got]).astype(BF16)
    for ref in sides:
        ref[base + n_row * marks :, :] = term


def chip_body(marks, near_ref, far_ref, *out):
    width = near_ref.shape[1]
    base = near_ref.shape[0] - marks - width
    size = base // len(out)
    term = (near_ref[base + marks :, :].astype(F32) + far_ref[base + marks :, :].astype(F32)).astype(BF16)
    for q, ref in enumerate(out):
        for side, src in enumerate((near_ref, far_ref)):
            ref[side * size : (side + 1) * size, :] = src[q * size : (q + 1) * size, :]
            at = 2 * size + side * marks
            ref[at : at + marks, :] = src[base : base + marks, :]
        ref[2 * size + 2 * marks :, :] = term


def product(dense_ref, first, grads, at, size):
    grad = jnp.concatenate([ref[...].T for ref in grads], axis=1)
    return dot(grad, dense_ref[first : first + grad.shape[1], at : at + size])


def backward_near_body(first, dense_ref, *refs):
    out = refs[-1]
    width = 2 * LANES
    for at in range(0, out.shape[1], width):
        size = min(width, out.shape[1] - at)
        out[:, at : at + size] = product(dense_ref, first, refs[:-1], at, size)


def backward_far_body(chips, dense_ref, near_ref, *refs):
    grads = refs[:chips]
    out = refs[chips:]
    rows = out[0].shape[0]
    width = 2 * LANES
    for at in range(0, near_ref.shape[1], width):
        size = min(width, near_ref.shape[1] - at)
        part = product(dense_ref, 0, grads, at, size) + near_ref[:, at : at + size]
        part = part.T.astype(BF16)
        for half in range(0, size, LANES):
            r, row = divmod(at + half, rows)
            out[r][row : row + LANES, :] = part[half : half + LANES, :]


def final_body(n_row, span, marks, scale, weight_ref, *refs):
    act_ref, total_ref, grad_ref = refs[-3:]
    parts = refs[:n_row]
    got = refs[n_row:-3]
    chips = len(got)
    rows, width = act_ref.shape
    lanes = 2 * chips * span
    size = n_row * span
    total_ref[...] = tree_sum([ref[2 * size + 2 * n_row * marks :, :] for ref in got]) * scale
    act = jnp.zeros((rows, width), F32)
    lane = iota((1, LANES), 1)
    for r in range(n_row):
        held = []
        for q in range(chips):
            for side in range(2):
                at = side * size + r * span
                held.append(got[q][at : at + span, :])
        held = jnp.concatenate(held, axis=0)
        for piece in range(lanes // LANES):
            place = jnp.zeros((1, LANES), F32)
            for k in range(2 * chips):
                at = k * span - piece * LANES
                if 0 <= at < LANES:
                    base = 2 * size + (k & 1) * n_row * marks + r * marks + 2 * piece
                    pair = got[k >> 1][base - base % 8 : base - base % 8 + 8, :].astype(F32)
                    high = pair[base % 8 : base % 8 + 1, :]
                    low = pair[base % 8 + 1 : base % 8 + 2, :]
                    inside = (lane >= at) & (lane < at + span)
                    place = jnp.where(inside, high * 128.0 + low, place)
            hot = (iota((rows, LANES), 0) + 1 == place.astype(I32)).astype(BF16)
            act = act + dot(hot, held[piece * LANES : (piece + 1) * LANES, :])
    act_ref[...] = act.astype(BF16)
    hidden = tree_sum([ref[...] for ref in parts])
    grad_ref[...] = dot(hidden.astype(BF16), weight_ref[...], 1, 1).astype(BF16)


def layer(features, weight, tiles, tile_dest, tile_src, tile_count, source_of, out_grad):
    rows, width = features.shape
    edge = tiles.shape[-1]
    n_row = lax.axis_size("row")
    n_col = lax.axis_size("col")
    n_all = n_row * n_col
    chips = n_col // 2
    span = -(-(rows // n_all) // 16) * 16
    slots = n_all * span
    lanes = n_col * span
    marks = -(-2 * (lanes // LANES) // 16) * 16
    sizes = (n_row, n_col, span)
    total = n_row * rows
    half = chips * rows
    vmem = pltpu.VMEM

    def row_swap(value, bit):
        return lax.ppermute(value, "row", xor_pairs(n_row, bit))

    def col_swap(value, bit):
        return lax.ppermute(value, "col", xor_pairs(n_col, bit))

    def row_swaps(values):
        return [values[0]] + [row_swap(values[k], k) for k in range(1, n_row)]

    def chip_swaps(values):
        return [values[0]] + [col_swap(values[k], 2 * k) for k in range(1, chips)]

    def block(count, kind=BF16, across=width):
        return jax.ShapeDtypeStruct((count, across), kind)

    dense_bytes = 4 * half * total
    kept = dense_bytes <= KEPT
    grant = GRANT if kept else dense_bytes + GRANT
    hbm = pltpu.HBM
    far_memory = lambda value: pltpu.with_memory_space_constraint(value, hbm)
    dense, own_table, slot, own_feat, own_cot = call(
        functools.partial(build_body, sizes),
        [
            pltpu.VMEM((2 * half, total), BF16) if kept else block(2 * half, BF16, total),
            block(8, I32, slots),
            block(8, I32, rows),
            block(rows),
            block(rows),
        ],
        (
            far_memory(tile_dest),
            far_memory(tile_src),
            tile_count,
            far_memory(source_of),
            far_memory(features),
            far_memory(out_grad),
            far_memory(tiles.reshape(tiles.shape[1:])),
        ),
        (hbm, hbm, pltpu.SMEM, hbm, hbm, hbm, hbm),
        scratch=[
            pltpu.SMEM(tile_dest.shape, I32),
            pltpu.SMEM(tile_src.shape, I32),
            pltpu.VMEM(source_of.shape, I32),
            pltpu.SMEM((2 * half // edge,), I32),
            pltpu.SMEM((total // edge,), I32),
            pltpu.SemaphoreType.DMA,
            pltpu.SemaphoreType.DMA((5,)),
        ],
        grant=grant,
        moved=tiles.size * 2,
    )
    table = own_table
    far_col = jnp.arange(slots)[None, :] // span % n_col
    bit = 1
    while bit < n_col:
        swapped = col_swap(table, bit)
        table = jnp.where(far_col & bit != 0, swapped, table)
        bit *= 2

    group = [own_feat] + row_swaps([features] * n_row)[1:]
    cotangent = [own_cot] + row_swaps([out_grad] * n_row)[1:]

    work = 2 * half * total * width
    far = call(
        functools.partial(forward_body, 0),
        block(half),
        (dense, *group),
        (vmem,) * (1 + n_row),
        grant=grant,
        flops=work,
    )
    got_far = col_swap(far, 1)
    near = call(
        functools.partial(forward_body, half),
        block(half),
        (dense, *group),
        (vmem,) * (1 + n_row),
        grant=grant,
        flops=work,
    )
    sums = call(
        combine_body, [block(rows)] * chips, (near, got_far), (vmem,) * 2, moved=half * width * 6
    )
    sums = chip_swaps(sums)

    near_cot, far_cot = call(
        functools.partial(pick_body, *sizes),
        [block(slots // 2)] * 2,
        (table, *cotangent),
        (vmem,) * (1 + n_row),
        flops=2 * slots * rows * width,
    )
    cot = call(
        pair_body,
        [block(slots // chips)] * chips,
        (near_cot, col_swap(far_cot, 1)),
        (vmem,) * 2,
        moved=slots * width * 4,
    )
    cot = chip_swaps(cot)

    grad, *sent = call(
        functools.partial(middle_body, n_row, chips),
        [block(rows)] + [block(lanes + marks + width)] * n_row,
        (slot, own_table, weight, *sums, *cot),
        (vmem,) * (3 + 2 * chips),
        flops=4 * slots * rows * width,
    )
    strip = chip_swaps([grad] * chips)
    other = [col_swap(value, 1) for value in strip]

    sent = row_swaps(sent)
    near_act, far_act = call(
        functools.partial(side_body, *sizes),
        [block(slots // 2 + n_row * marks + width)] * 2,
        sent,
        (vmem,) * n_row,
        moved=slots * width * 4,
    )
    by_chip = call(
        functools.partial(chip_body, n_row * marks),
        [block(slots // chips + 2 * n_row * marks + width)] * chips,
        (near_act, col_swap(far_act, 1)),
        (vmem,) * 2,
        moved=slots * width * 4,
    )
    by_chip = chip_swaps(by_chip)

    part = call(
        functools.partial(backward_near_body, half),
        block(width, F32, total),
        (dense, *strip),
        (vmem,) * (1 + chips),
        grant=grant,
        flops=work,
    )
    part = call(
        functools.partial(backward_far_body, chips),
        [block(rows)] * n_row,
        (dense, part, *other),
        (vmem,) * (2 + chips),
        grant=grant,
        flops=work,
    )
    part = row_swaps(part)
    activations, weight_grad, feature_grad = call(
        functools.partial(final_body, n_row, span, marks, 1.0 / math.sqrt(rows * n_all)),
        [block(rows), block(width, F32), block(rows)],
        (weight, *part, *by_chip),
        (vmem,) * (1 + n_row + chips),
        flops=2 * (slots + width) * rows * width,
    )
    return (activations, feature_grad, weight_grad)


def solution(mesh):
    placed = (
        P(("row", "col"), None),
        P(),
        P("row", "col", None, None),
        P("row", "col"),
        P("row", "col"),
        P("row", "col"),
        P(("row", "col")),
        P(("row", "col"), None),
    )
    return jax.shard_map(
        layer,
        mesh=mesh,
        in_specs=placed,
        out_specs=(P(("row", "col"), None), P(("row", "col"), None), P()),
        check_vma=False,
    )
```

```python
import functools
import math

import jax
import jax.numpy as jnp
from jax import lax
from jax.experimental import pallas as pl
from jax.experimental.pallas import tpu as pltpu
from jax.sharding import PartitionSpec as P


BF16 = jnp.bfloat16
F32 = jnp.float32
I32 = jnp.int32
LANES = 128
GRANT = 16 << 20
KEPT = 24 << 20


def xor_pairs(size, bit):
    return [(i, i ^ bit) for i in range(size)]


def dot(a, b, left=1, right=0):
    return lax.dot_general(a, b, (((left,), (right,)), ((), ())), preferred_element_type=F32)


def iota(shape, dim):
    return lax.broadcasted_iota(I32, shape, dim)


def call(body, out_shape, operands, spaces, scratch=(), flops=0, moved=0, grant=GRANT):
    single = not isinstance(out_shape, (list, tuple))
    spec = pl.BlockSpec(memory_space=pltpu.VMEM)
    return pl.pallas_call(
        body,
        out_shape=out_shape,
        in_specs=[pl.BlockSpec(memory_space=space) for space in spaces],
        out_specs=spec if single else [spec] * len(out_shape),
        scratch_shapes=list(scratch),
        compiler_params=pltpu.CompilerParams(vmem_limit_bytes=grant),
        cost_estimate=pl.CostEstimate(flops=flops, bytes_accessed=moved, transcendentals=0),
    )(*operands)


def half_place(part, me, chips):
    far = part ^ me
    return (1 - (far & 1)) * chips + (far >> 1)


def build_body(
    sizes,
    dest_hbm,
    src_hbm,
    count_ref,
    source_hbm,
    feat_hbm,
    cot_hbm,
    tiles_ref,
    dense_ref,
    table_ref,
    other_ref,
    slot_ref,
    feat_ref,
    cot_ref,
    dest_ref,
    src_ref,
    source_ref,
    row_ref,
    col_ref,
    sem,
    near,
):
    n_row, n_col, span = sizes
    edge = tiles_ref.shape[-1]
    rows, cols = dense_ref.shape
    per = cols // (n_row * edge)
    chunk = 2 * edge
    my_row = lax.axis_index("row")
    my_col = lax.axis_index("col")
    loads = [
        pltpu.make_async_copy(dest_hbm, dest_ref, near.at[0]),
        pltpu.make_async_copy(src_hbm, src_ref, near.at[1]),
        pltpu.make_async_copy(source_hbm, source_ref, near.at[2]),
    ]
    rows_in = [
        pltpu.make_async_copy(feat_hbm, feat_ref, near.at[3]),
        pltpu.make_async_copy(cot_hbm, cot_ref, near.at[4]),
    ]
    for load in loads + rows_in:
        load.start()
    for part in range(n_col):
        for block in range(per):
            row_ref[part * per + block] = (half_place(part, my_col, n_col // 2) * per + block) * edge
    for part in range(n_row):
        for block in range(per):
            col_ref[part * per + block] = ((part ^ my_row) * per + block) * edge

    def clear(step, carry):
        at = pl.multiple_of(step * chunk, chunk)
        dense_ref[pl.ds(at, chunk), :] = jnp.zeros((chunk, cols), BF16)
        return carry

    lax.fori_loop(0, rows // chunk, clear, 0)
    for load in loads:
        load.wait()
    live = count_ref[0, 0]

    def start(slot):
        row = pl.multiple_of(row_ref[dest_ref[0, slot]], edge)
        col = pl.multiple_of(col_ref[src_ref[0, slot]], edge)
        pltpu.make_async_copy(
            tiles_ref.at[slot], dense_ref.at[pl.ds(row, edge), pl.ds(col, edge)], sem
        ).start()

    def start_some(step, carry):
        for at in range(4):
            start(step * 4 + at)
        return carry

    def start_one(slot, carry):
        start(slot)
        return carry

    some = live >> 2
    lax.fori_loop(0, some, start_some, 0)
    lax.fori_loop(some * 4, live, start_one, 0)

    slot_work(n_row, n_col, span, source_ref, table_ref, other_ref, slot_ref)
    for load in rows_in:
        load.wait()

    def arrived(count):
        part = dense_ref.at[pl.ds(0, edge), pl.ds(0, count * edge)]
        return pltpu.make_async_copy(part, part, sem)

    def wait_many(step, carry):
        arrived(8).wait()
        return carry

    def wait_one(step, carry):
        arrived(1).wait()
        return carry

    lax.fori_loop(0, live >> 3, wait_many, 0)
    lax.fori_loop(0, live & 7, wait_one, 0)


def slot_work(n_row, n_col, span, source_ref, table_ref, other_ref, slot_ref):
    rows = source_ref.shape[-1]
    slots = table_ref.shape[-1]
    n_all = n_row * n_col
    my_row = lax.axis_index("row")
    my_col = lax.axis_index("col")
    source = source_ref[...].reshape(1, rows)
    owner = ((source.astype(F32) + 0.5) * (1.0 / rows)).astype(I32)
    place = source - owner * rows + 1
    mine = iota((n_all, rows), 0) == owner
    before = (iota((rows, rows), 0) < iota((rows, rows), 1)).astype(BF16)
    earlier = dot(mine.astype(BF16), before)
    rank = jnp.sum(jnp.where(mine, earlier, 0.0), axis=0, keepdims=True).astype(I32)
    shift = n_col.bit_length() - 1
    far_row = (owner >> shift) ^ my_row
    far_col = (owner & (n_col - 1)) ^ my_col
    by_row = (far_row * n_col + far_col) * span + rank
    by_col = (far_col * n_row + far_row) * span + rank
    high = jnp.broadcast_to((place >> 7).astype(F32), (8, rows)).astype(BF16)
    low = jnp.broadcast_to((place & 127).astype(F32), (8, rows)).astype(BF16)
    for ref, order in ((table_ref, by_row), (other_ref, by_col)):
        hot = (iota((slots, rows), 0) == order).astype(BF16)
        ref[...] = (dot(high, hot, 1, 1) * 128.0 + dot(low, hot, 1, 1)).astype(I32)
    slot_ref[...] = jnp.broadcast_to(by_row, (8, rows))


def pick_body(n_row, n_col, span, table_ref, *refs):
    cot = refs[:n_col]
    out = refs[n_col:]
    rows = cot[0].shape[0]
    tail = n_row * span
    for base in range(0, n_col * tail, LANES):
        place = table_ref[0:1, base : base + LANES]
        hot = (iota((rows, LANES), 0) + 1 == place).astype(BF16)
        for k in range(base // tail, -(-(base + LANES) // tail)):
            picked = dot(hot, cot[(k >> 1) + (k & 1) * (n_col // 2)][...], 0, 0).astype(BF16)
            for r in range(n_row):
                at = k * tail + r * span - base
                if 0 <= at < LANES:
                    out[r][k * span : (k + 1) * span, :] = picked[at : at + span, :]


def tree_sum(terms):
    terms = [term.astype(F32) for term in terms]
    while len(terms) > 1:
        terms = [terms[at] + terms[at + 1] for at in range(0, len(terms), 2)]
    return terms[0]


def forward_body(first, dense_ref, *refs):
    out = refs[-1]
    feat = jnp.concatenate([ref[...] for ref in refs[:-1]], axis=0)
    count = out.shape[0]
    step = 512 if count % 512 == 0 else 128
    for at in range(0, count, step):
        out[at : at + step, :] = dot(dense_ref[first + at : first + at + step, :], feat).astype(BF16)


def combine_body(own_ref, got_ref, *out):
    rows = out[0].shape[0]
    for at, ref in enumerate(out):
        part = slice(at * rows, (at + 1) * rows)
        ref[...] = (own_ref[part, :].astype(F32) + got_ref[part, :].astype(F32)).astype(BF16)


def middle_body(n_row, chips, slot_ref, table_ref, weight_ref, *refs):
    got = refs[:chips]
    back = refs[chips : chips + n_row]
    grad_ref = refs[chips + n_row]
    out = refs[chips + n_row + 1 :]
    rows, width = grad_ref.shape
    slots = table_ref.shape[1]
    lanes = slots // n_row
    marks = out[0].shape[0] - lanes - width
    mixed = got[0][...].astype(F32)
    for ref in got[1:]:
        mixed = mixed + ref[...].astype(F32)
    mixed = mixed.astype(BF16)
    pre = dot(mixed, weight_ref[...]).astype(BF16).astype(F32)
    sigma = jax.nn.sigmoid(pre)
    act = (pre * sigma).astype(BF16)
    returned = jnp.concatenate([ref[...] for ref in back], axis=0)
    hot = (iota((slots, rows), 0) == slot_ref[0:1, :]).astype(BF16)
    dest_grad = dot(hot, returned, 0, 0)
    grad = (dest_grad * (sigma * (1.0 + pre * (1.0 - sigma)))).astype(BF16)
    grad_ref[...] = grad
    sent = dot(hot, act).astype(BF16)
    term = dot(mixed, grad, 0, 0).astype(BF16)
    row = iota((marks, LANES), 0)
    for r in range(n_row):
        out[r][:lanes, :] = sent[r * lanes : (r + 1) * lanes, :]
        block = jnp.zeros((marks, LANES), F32)
        for piece in range(lanes // LANES):
            at = r * lanes + piece * LANES
            place = table_ref[0:1, at : at + LANES]
            block = jnp.where(row == 2 * piece, (place >> 7).astype(F32), block)
            block = jnp.where(row == 2 * piece + 1, (place & 127).astype(F32), block)
        out[r][lanes : lanes + marks, :] = block.astype(BF16)
        out[r][lanes + marks :, :] = term


def side_body(n_row, n_col, span, *refs):
    got = refs[:n_row]
    sides = refs[n_row:]
    lanes = n_col * span
    width = got[0].shape[1]
    marks = got[0].shape[0] - lanes - width
    base = lanes * n_row // 2
    for r in range(n_row):
        for k in range(n_col):
            at = ((k >> 1) * n_row + r) * span
            sides[k & 1][at : at + span, :] = got[r][k * span : (k + 1) * span, :]
        for ref in sides:
            at = base + r * marks
            ref[at : at + marks, :] = got[r][lanes : lanes + marks, :]
    term = tree_sum([ref[lanes + marks :, :] for ref in got]).astype(BF16)
    for ref in sides:
        ref[base + n_row * marks :, :] = term


def chip_body(marks, near_ref, far_ref, *out):
    width = near_ref.shape[1]
    base = near_ref.shape[0] - marks - width
    size = base // len(out)
    term = (near_ref[base + marks :, :].astype(F32) + far_ref[base + marks :, :].astype(F32)).astype(BF16)
    for q, ref in enumerate(out):
        for side, src in enumerate((near_ref, far_ref)):
            ref[side * size : (side + 1) * size, :] = src[q * size : (q + 1) * size, :]
            at = 2 * size + side * marks
            ref[at : at + marks, :] = src[base : base + marks, :]
        ref[2 * size + 2 * marks :, :] = term


def product(dense_ref, first, grads, at, size):
    grad = jnp.concatenate([ref[...].T for ref in grads], axis=1)
    return dot(grad, dense_ref[first : first + grad.shape[1], at : at + size])


def backward_near_body(first, dense_ref, *refs):
    out = refs[-1]
    width = 2 * LANES
    for at in range(0, out.shape[1], width):
        size = min(width, out.shape[1] - at)
        out[:, at : at + size] = product(dense_ref, first, refs[:-1], at, size)


def backward_far_body(chips, dense_ref, near_ref, *refs):
    grads = refs[:chips]
    out = refs[chips:]
    rows = out[0].shape[0]
    width = 2 * LANES
    for at in range(0, near_ref.shape[1], width):
        size = min(width, near_ref.shape[1] - at)
        part = product(dense_ref, 0, grads, at, size) + near_ref[:, at : at + size]
        part = part.T.astype(BF16)
        for half in range(0, size, LANES):
            r, row = divmod(at + half, rows)
            out[r][row : row + LANES, :] = part[half : half + LANES, :]


def final_body(n_row, span, marks, scale, weight_ref, *refs):
    act_ref, total_ref, grad_ref = refs[-3:]
    parts = refs[:n_row]
    got = refs[n_row:-3]
    chips = len(got)
    rows, width = act_ref.shape
    lanes = 2 * chips * span
    size = n_row * span
    total_ref[...] = tree_sum([ref[2 * size + 2 * n_row * marks :, :] for ref in got]) * scale
    act = jnp.zeros((rows, width), F32)
    lane = iota((1, LANES), 1)
    for r in range(n_row):
        held = []
        for q in range(chips):
            for side in range(2):
                at = side * size + r * span
                held.append(got[q][at : at + span, :])
        held = jnp.concatenate(held, axis=0)
        for piece in range(lanes // LANES):
            place = jnp.zeros((1, LANES), F32)
            for k in range(2 * chips):
                at = k * span - piece * LANES
                if 0 <= at < LANES:
                    base = 2 * size + (k & 1) * n_row * marks + r * marks + 2 * piece
                    pair = got[k >> 1][base - base % 8 : base - base % 8 + 8, :].astype(F32)
                    high = pair[base % 8 : base % 8 + 1, :]
                    low = pair[base % 8 + 1 : base % 8 + 2, :]
                    inside = (lane >= at) & (lane < at + span)
                    place = jnp.where(inside, high * 128.0 + low, place)
            hot = (iota((rows, LANES), 0) + 1 == place.astype(I32)).astype(BF16)
            act = act + dot(hot, held[piece * LANES : (piece + 1) * LANES, :])
    act_ref[...] = act.astype(BF16)
    hidden = tree_sum([ref[...] for ref in parts])
    grad_ref[...] = dot(hidden.astype(BF16), weight_ref[...], 1, 1).astype(BF16)


def layer(features, weight, tiles, tile_dest, tile_src, tile_count, source_of, out_grad):
    rows, width = features.shape
    edge = tiles.shape[-1]
    n_row = lax.axis_size("row")
    n_col = lax.axis_size("col")
    n_all = n_row * n_col
    chips = n_col // 2
    span = -(-(rows // n_all) // 16) * 16
    slots = n_all * span
    lanes = n_col * span
    marks = -(-2 * (lanes // LANES) // 16) * 16
    sizes = (n_row, n_col, span)
    total = n_row * rows
    half = chips * rows
    vmem = pltpu.VMEM

    def row_swap(value, bit):
        return lax.ppermute(value, "row", xor_pairs(n_row, bit))

    def col_swap(value, bit):
        return lax.ppermute(value, "col", xor_pairs(n_col, bit))

    def row_swaps(values):
        return [values[0]] + [row_swap(values[k], k) for k in range(1, n_row)]

    def chip_swaps(values):
        return [values[0]] + [col_swap(values[k], 2 * k) for k in range(1, chips)]

    def block(count, kind=BF16, across=width):
        return jax.ShapeDtypeStruct((count, across), kind)

    dense_bytes = 4 * half * total
    kept = dense_bytes <= KEPT
    grant = GRANT if kept else dense_bytes + GRANT
    hbm = pltpu.HBM
    far_memory = lambda value: pltpu.with_memory_space_constraint(value, hbm)
    dense, own_table, table, slot, own_feat, own_cot = call(
        functools.partial(build_body, sizes),
        [
            pltpu.VMEM((2 * half, total), BF16) if kept else block(2 * half, BF16, total),
            block(8, I32, slots),
            block(8, I32, slots),
            block(8, I32, rows),
            block(rows),
            block(rows),
        ],
        (
            far_memory(tile_dest),
            far_memory(tile_src),
            tile_count,
            far_memory(source_of),
            far_memory(features),
            far_memory(out_grad),
            far_memory(tiles.reshape(tiles.shape[1:])),
        ),
        (hbm, hbm, pltpu.SMEM, hbm, hbm, hbm, hbm),
        scratch=[
            pltpu.SMEM(tile_dest.shape, I32),
            pltpu.SMEM(tile_src.shape, I32),
            pltpu.VMEM(source_of.shape, I32),
            pltpu.SMEM((2 * half // edge,), I32),
            pltpu.SMEM((total // edge,), I32),
            pltpu.SemaphoreType.DMA,
            pltpu.SemaphoreType.DMA((5,)),
        ],
        grant=grant,
        moved=tiles.size * 2,
    )
    far_row = jnp.arange(slots)[None, :] // span % n_row
    bit = 1
    while bit < n_row:
        swapped = row_swap(table, bit)
        table = jnp.where(far_row & bit != 0, swapped, table)
        bit *= 2

    group = [own_feat] + row_swaps([features] * n_row)[1:]
    cotangent = [own_cot] + chip_swaps([out_grad] * chips)[1:]
    cotangent += [col_swap(value, 1) for value in cotangent]

    work = 2 * half * total * width
    far = call(
        functools.partial(forward_body, 0),
        block(half),
        (dense, *group),
        (vmem,) * (1 + n_row),
        grant=grant,
        flops=work,
    )
    got_far = col_swap(far, 1)
    near = call(
        functools.partial(forward_body, half),
        block(half),
        (dense, *group),
        (vmem,) * (1 + n_row),
        grant=grant,
        flops=work,
    )
    sums = call(
        combine_body, [block(rows)] * chips, (near, got_far), (vmem,) * 2, moved=half * width * 6
    )
    sums = chip_swaps(sums)

    cot = call(
        functools.partial(pick_body, *sizes),
        [block(lanes)] * n_row,
        (table, *cotangent),
        (vmem,) * (1 + n_col),
        flops=4 * slots * rows * width,
    )
    cot = row_swaps(cot)

    grad, *sent = call(
        functools.partial(middle_body, n_row, chips),
        [block(rows)] + [block(lanes + marks + width)] * n_row,
        (slot, own_table, weight, *sums, *cot),
        (vmem,) * (3 + chips + n_row),
        flops=4 * slots * rows * width,
    )
    strip = chip_swaps([grad] * chips)
    other = [col_swap(value, 1) for value in strip]

    sent = row_swaps(sent)
    near_act, far_act = call(
        functools.partial(side_body, *sizes),
        [block(slots // 2 + n_row * marks + width)] * 2,
        sent,
        (vmem,) * n_row,
        moved=slots * width * 4,
    )
    by_chip = call(
        functools.partial(chip_body, n_row * marks),
        [block(slots // chips + 2 * n_row * marks + width)] * chips,
        (near_act, col_swap(far_act, 1)),
        (vmem,) * 2,
        moved=slots * width * 4,
    )
    by_chip = chip_swaps(by_chip)

    part = call(
        functools.partial(backward_near_body, half),
        block(width, F32, total),
        (dense, *strip),
        (vmem,) * (1 + chips),
        grant=grant,
        flops=work,
    )
    part = call(
        functools.partial(backward_far_body, chips),
        [block(rows)] * n_row,
        (dense, part, *other),
        (vmem,) * (2 + chips),
        grant=grant,
        flops=work,
    )
    part = row_swaps(part)
    activations, weight_grad, feature_grad = call(
        functools.partial(final_body, n_row, span, marks, 1.0 / math.sqrt(rows * n_all)),
        [block(rows), block(width, F32), block(rows)],
        (weight, *part, *by_chip),
        (vmem,) * (1 + n_row + chips),
        flops=2 * (slots + width) * rows * width,
    )
    return (activations, feature_grad, weight_grad)


def solution(mesh):
    placed = (
        P(("row", "col"), None),
        P(),
        P("row", "col", None, None),
        P("row", "col"),
        P("row", "col"),
        P("row", "col"),
        P(("row", "col")),
        P(("row", "col"), None),
    )
    return jax.shard_map(
        layer,
        mesh=mesh,
        in_specs=placed,
        out_specs=(P(("row", "col"), None), P(("row", "col"), None), P()),
        check_vma=False,
    )
```

```python
import functools
import math

import jax
import jax.numpy as jnp
from jax import lax
from jax.experimental import pallas as pl
from jax.experimental.pallas import tpu as pltpu
from jax.sharding import PartitionSpec as P


BF16 = jnp.bfloat16
F32 = jnp.float32
I32 = jnp.int32
LANES = 128
GRANT = 16 << 20
KEPT = 24 << 20


def xor_pairs(size, bit):
    return [(i, i ^ bit) for i in range(size)]


def dot(a, b, left=1, right=0):
    return lax.dot_general(a, b, (((left,), (right,)), ((), ())), preferred_element_type=F32)


def iota(shape, dim):
    return lax.broadcasted_iota(I32, shape, dim)


def call(body, out_shape, operands, spaces, scratch=(), flops=0, moved=0, grant=GRANT):
    single = not isinstance(out_shape, (list, tuple))
    spec = pl.BlockSpec(memory_space=pltpu.VMEM)
    return pl.pallas_call(
        body,
        out_shape=out_shape,
        in_specs=[pl.BlockSpec(memory_space=space) for space in spaces],
        out_specs=spec if single else [spec] * len(out_shape),
        scratch_shapes=list(scratch),
        compiler_params=pltpu.CompilerParams(vmem_limit_bytes=grant),
        cost_estimate=pl.CostEstimate(flops=flops, bytes_accessed=moved, transcendentals=0),
    )(*operands)


def half_place(part, me, chips):
    far = part ^ me
    return (1 - (far & 1)) * chips + (far >> 1)


def build_body(
    sizes,
    dest_hbm,
    src_hbm,
    count_ref,
    source_hbm,
    feat_hbm,
    cot_hbm,
    tiles_ref,
    dense_ref,
    table_ref,
    other_ref,
    slot_ref,
    feat_ref,
    cot_ref,
    dest_ref,
    src_ref,
    source_ref,
    row_ref,
    col_ref,
    sem,
    near,
):
    n_row, n_col, span = sizes
    edge = tiles_ref.shape[-1]
    rows, cols = dense_ref.shape
    per = cols // (n_row * edge)
    chunk = 2 * edge
    my_row = lax.axis_index("row")
    my_col = lax.axis_index("col")
    loads = [
        pltpu.make_async_copy(dest_hbm, dest_ref, near.at[0]),
        pltpu.make_async_copy(src_hbm, src_ref, near.at[1]),
        pltpu.make_async_copy(source_hbm, source_ref, near.at[2]),
    ]
    rows_in = [
        pltpu.make_async_copy(feat_hbm, feat_ref, near.at[3]),
        pltpu.make_async_copy(cot_hbm, cot_ref, near.at[4]),
    ]
    for load in loads + rows_in:
        load.start()
    for part in range(n_col):
        for block in range(per):
            row_ref[part * per + block] = (half_place(part, my_col, n_col // 2) * per + block) * edge
    for part in range(n_row):
        for block in range(per):
            col_ref[part * per + block] = ((part ^ my_row) * per + block) * edge

    def clear(step, carry):
        at = pl.multiple_of(step * chunk, chunk)
        dense_ref[pl.ds(at, chunk), :] = jnp.zeros((chunk, cols), BF16)
        return carry

    lax.fori_loop(0, rows // chunk, clear, 0)
    for load in loads:
        load.wait()
    live = count_ref[0, 0]

    def start(slot):
        row = pl.multiple_of(row_ref[dest_ref[0, slot]], edge)
        col = pl.multiple_of(col_ref[src_ref[0, slot]], edge)
        pltpu.make_async_copy(
            tiles_ref.at[slot], dense_ref.at[pl.ds(row, edge), pl.ds(col, edge)], sem
        ).start()

    def start_some(step, carry):
        for at in range(4):
            start(step * 4 + at)
        return carry

    def start_one(slot, carry):
        start(slot)
        return carry

    some = live >> 2
    lax.fori_loop(0, some, start_some, 0)
    lax.fori_loop(some * 4, live, start_one, 0)

    slot_work(n_row, n_col, span, source_ref, table_ref, other_ref, slot_ref)
    for load in rows_in:
        load.wait()

    def arrived(count):
        part = dense_ref.at[pl.ds(0, edge), pl.ds(0, count * edge)]
        return pltpu.make_async_copy(part, part, sem)

    def wait_many(step, carry):
        arrived(8).wait()
        return carry

    def wait_one(step, carry):
        arrived(1).wait()
        return carry

    lax.fori_loop(0, live >> 3, wait_many, 0)
    lax.fori_loop(0, live & 7, wait_one, 0)


def slot_work(n_row, n_col, span, source_ref, table_ref, other_ref, slot_ref):
    rows = source_ref.shape[-1]
    slots = table_ref.shape[-1]
    n_all = n_row * n_col
    my_row = lax.axis_index("row")
    my_col = lax.axis_index("col")
    source = source_ref[...].reshape(1, rows)
    owner = ((source.astype(F32) + 0.5) * (1.0 / rows)).astype(I32)
    place = source - owner * rows + 1
    mine = iota((n_all, rows), 0) == owner
    before = (iota((rows, rows), 0) < iota((rows, rows), 1)).astype(BF16)
    earlier = dot(mine.astype(BF16), before)
    rank = jnp.sum(jnp.where(mine, earlier, 0.0), axis=0, keepdims=True).astype(I32)
    shift = n_col.bit_length() - 1
    far_row = (owner >> shift) ^ my_row
    far_col = (owner & (n_col - 1)) ^ my_col
    by_row = (far_row * n_col + far_col) * span + rank
    by_col = (far_col * n_row + far_row) * span + rank
    high = jnp.broadcast_to((place >> 7).astype(F32), (8, rows)).astype(BF16)
    low = jnp.broadcast_to((place & 127).astype(F32), (8, rows)).astype(BF16)
    for ref, order in ((table_ref, by_row), (other_ref, by_col)):
        hot = (iota((slots, rows), 0) == order).astype(BF16)
        ref[...] = (dot(high, hot, 1, 1) * 128.0 + dot(low, hot, 1, 1)).astype(I32)
    slot_ref[...] = jnp.broadcast_to(by_row, (8, rows))


def pick_body(n_row, n_col, span, table_ref, *refs):
    cot = refs[:n_col]
    out = refs[n_col:]
    rows = cot[0].shape[0]
    tail = n_row * span
    for base in range(0, n_col * tail, LANES):
        place = table_ref[0:1, base : base + LANES]
        hot = (iota((rows, LANES), 0) + 1 == place).astype(BF16)
        for k in range(base // tail, -(-(base + LANES) // tail)):
            picked = dot(hot, cot[(k >> 1) + (k & 1) * (n_col // 2)][...], 0, 0).astype(BF16)
            for r in range(n_row):
                at = k * tail + r * span - base
                if 0 <= at < LANES:
                    out[r][k * span : (k + 1) * span, :] = picked[at : at + span, :]


def tree_sum(terms):
    terms = [term.astype(F32) for term in terms]
    while len(terms) > 1:
        terms = [terms[at] + terms[at + 1] for at in range(0, len(terms), 2)]
    return terms[0]


def forward_body(first, dense_ref, *refs):
    out = refs[-1]
    feat = jnp.concatenate([ref[...] for ref in refs[:-1]], axis=0)
    count = out.shape[0]
    step = 512 if count % 512 == 0 else 128
    for at in range(0, count, step):
        out[at : at + step, :] = dot(dense_ref[first + at : first + at + step, :], feat).astype(BF16)


def combine_body(own_ref, got_ref, *out):
    rows = out[0].shape[0]
    for at, ref in enumerate(out):
        part = slice(at * rows, (at + 1) * rows)
        ref[...] = (own_ref[part, :].astype(F32) + got_ref[part, :].astype(F32)).astype(BF16)


def middle_body(n_row, chips, slot_ref, table_ref, weight_ref, *refs):
    got = refs[:chips]
    back = refs[chips : chips + n_row]
    grad_ref = refs[chips + n_row]
    out = refs[chips + n_row + 1 :]
    rows, width = grad_ref.shape
    slots = table_ref.shape[1]
    lanes = slots // n_row
    marks = out[0].shape[0] - lanes - width
    mixed = got[0][...].astype(F32)
    for ref in got[1:]:
        mixed = mixed + ref[...].astype(F32)
    mixed = mixed.astype(BF16)
    pre = dot(mixed, weight_ref[...]).astype(BF16).astype(F32)
    sigma = jax.nn.sigmoid(pre)
    act = (pre * sigma).astype(BF16)
    returned = jnp.concatenate([ref[...] for ref in back], axis=0)
    hot = (iota((slots, rows), 0) == slot_ref[0:1, :]).astype(BF16)
    dest_grad = dot(hot, returned, 0, 0)
    grad = (dest_grad * (sigma * (1.0 + pre * (1.0 - sigma)))).astype(BF16)
    grad_ref[...] = grad
    sent = dot(hot, act).astype(BF16)
    term = dot(mixed, grad, 0, 0).astype(BF16)
    row = iota((marks, LANES), 0)
    for r in range(n_row):
        out[r][:lanes, :] = sent[r * lanes : (r + 1) * lanes, :]
        block = jnp.zeros((marks, LANES), F32)
        for piece in range(lanes // LANES):
            at = r * lanes + piece * LANES
            place = table_ref[0:1, at : at + LANES]
            block = jnp.where(row == 2 * piece, (place >> 7).astype(F32), block)
            block = jnp.where(row == 2 * piece + 1, (place & 127).astype(F32), block)
        out[r][lanes : lanes + marks, :] = block.astype(BF16)
        out[r][lanes + marks :, :] = term


def side_body(n_row, n_col, span, all_marks, *refs):
    got = refs[:n_row]
    sides = refs[n_row:]
    lanes = n_col * span
    width = got[0].shape[1]
    marks = got[0].shape[0] - lanes - width
    base = lanes * n_row // 2
    lines = 2 * (lanes // LANES)
    row = iota((all_marks, LANES), 0)
    block = jnp.zeros((all_marks, LANES), F32)
    for r in range(n_row):
        for k in range(n_col):
            at = ((k >> 1) * n_row + r) * span
            sides[k & 1][at : at + span, :] = got[r][k * span : (k + 1) * span, :]
        held = got[r][lanes : lanes + marks, :].astype(F32)
        for line in range(lines):
            block = jnp.where(row == r * lines + line, held[line : line + 1, :], block)
    term = tree_sum([ref[lanes + marks :, :] for ref in got]).astype(BF16)
    for ref in sides:
        ref[base : base + all_marks, :] = block.astype(BF16)
        ref[base + all_marks :, :] = term


def chip_body(marks, near_ref, far_ref, *out):
    width = near_ref.shape[1]
    base = near_ref.shape[0] - marks - width
    size = base // len(out)
    term = (near_ref[base + marks :, :].astype(F32) + far_ref[base + marks :, :].astype(F32)).astype(BF16)
    for q, ref in enumerate(out):
        for side, src in enumerate((near_ref, far_ref)):
            ref[side * size : (side + 1) * size, :] = src[q * size : (q + 1) * size, :]
            at = 2 * size + side * marks
            ref[at : at + marks, :] = src[base : base + marks, :]
        ref[2 * size + 2 * marks :, :] = term


def product(dense_ref, first, grads, at, size):
    grad = jnp.concatenate([ref[...].T for ref in grads], axis=1)
    return dot(grad, dense_ref[first : first + grad.shape[1], at : at + size])


def backward_near_body(first, dense_ref, *refs):
    out = refs[-1]
    width = 2 * LANES
    for at in range(0, out.shape[1], width):
        size = min(width, out.shape[1] - at)
        out[:, at : at + size] = product(dense_ref, first, refs[:-1], at, size)


def backward_far_body(chips, dense_ref, near_ref, *refs):
    grads = refs[:chips]
    out = refs[chips:]
    rows = out[0].shape[0]
    width = 2 * LANES
    for at in range(0, near_ref.shape[1], width):
        size = min(width, near_ref.shape[1] - at)
        part = product(dense_ref, 0, grads, at, size) + near_ref[:, at : at + size]
        part = part.T.astype(BF16)
        for half in range(0, size, LANES):
            r, row = divmod(at + half, rows)
            out[r][row : row + LANES, :] = part[half : half + LANES, :]


def final_body(n_row, span, all_marks, scale, weight_ref, *refs):
    act_ref, total_ref, grad_ref = refs[-3:]
    parts = refs[:n_row]
    got = refs[n_row:-3]
    chips = len(got)
    rows, width = act_ref.shape
    lanes = 2 * chips * span
    size = n_row * span
    total_ref[...] = tree_sum([ref[2 * size + 2 * all_marks :, :] for ref in got]) * scale
    act = jnp.zeros((rows, width), F32)
    lane = iota((1, LANES), 1)
    for r in range(n_row):
        held = []
        for q in range(chips):
            for side in range(2):
                at = side * size + r * span
                held.append(got[q][at : at + span, :])
        held = jnp.concatenate(held, axis=0)
        for piece in range(lanes // LANES):
            place = jnp.zeros((1, LANES), F32)
            for k in range(2 * chips):
                at = k * span - piece * LANES
                if 0 <= at < LANES:
                    base = 2 * size + (k & 1) * all_marks + 2 * (r * (lanes // LANES) + piece)
                    pair = got[k >> 1][base - base % 8 : base - base % 8 + 8, :].astype(F32)
                    high = pair[base % 8 : base % 8 + 1, :]
                    low = pair[base % 8 + 1 : base % 8 + 2, :]
                    inside = (lane >= at) & (lane < at + span)
                    place = jnp.where(inside, high * 128.0 + low, place)
            hot = (iota((rows, LANES), 0) + 1 == place.astype(I32)).astype(BF16)
            act = act + dot(hot, held[piece * LANES : (piece + 1) * LANES, :])
    act_ref[...] = act.astype(BF16)
    hidden = tree_sum([ref[...] for ref in parts])
    grad_ref[...] = dot(hidden.astype(BF16), weight_ref[...], 1, 1).astype(BF16)


def layer(features, weight, tiles, tile_dest, tile_src, tile_count, source_of, out_grad):
    rows, width = features.shape
    edge = tiles.shape[-1]
    n_row = lax.axis_size("row")
    n_col = lax.axis_size("col")
    n_all = n_row * n_col
    chips = n_col // 2
    span = -(-(rows // n_all) // 16) * 16
    slots = n_all * span
    lanes = n_col * span
    marks = -(-2 * (lanes // LANES) // 16) * 16
    all_marks = -(-2 * (slots // LANES) // 16) * 16
    sizes = (n_row, n_col, span)
    total = n_row * rows
    half = chips * rows
    vmem = pltpu.VMEM

    def row_swap(value, bit):
        return lax.ppermute(value, "row", xor_pairs(n_row, bit))

    def col_swap(value, bit):
        return lax.ppermute(value, "col", xor_pairs(n_col, bit))

    def row_swaps(values):
        return [values[0]] + [row_swap(values[k], k) for k in range(1, n_row)]

    def chip_swaps(values):
        return [values[0]] + [col_swap(values[k], 2 * k) for k in range(1, chips)]

    def block(count, kind=BF16, across=width):
        return jax.ShapeDtypeStruct((count, across), kind)

    dense_bytes = 4 * half * total
    kept = dense_bytes <= KEPT
    grant = GRANT if kept else dense_bytes + GRANT
    hbm = pltpu.HBM
    far_memory = lambda value: pltpu.with_memory_space_constraint(value, hbm)
    dense, own_table, table, slot, own_feat, own_cot = call(
        functools.partial(build_body, sizes),
        [
            pltpu.VMEM((2 * half, total), BF16) if kept else block(2 * half, BF16, total),
            block(8, I32, slots),
            block(8, I32, slots),
            block(8, I32, rows),
            block(rows),
            block(rows),
        ],
        (
            far_memory(tile_dest),
            far_memory(tile_src),
            tile_count,
            far_memory(source_of),
            far_memory(features),
            far_memory(out_grad),
            far_memory(tiles.reshape(tiles.shape[1:])),
        ),
        (hbm, hbm, pltpu.SMEM, hbm, hbm, hbm, hbm),
        scratch=[
            pltpu.SMEM(tile_dest.shape, I32),
            pltpu.SMEM(tile_src.shape, I32),
            pltpu.VMEM(source_of.shape, I32),
            pltpu.SMEM((2 * half // edge,), I32),
            pltpu.SMEM((total // edge,), I32),
            pltpu.SemaphoreType.DMA,
            pltpu.SemaphoreType.DMA((5,)),
        ],
        grant=grant,
        moved=tiles.size * 2,
    )
    far_row = jnp.arange(slots)[None, :] // span % n_row
    bit = 1
    while bit < n_row:
        swapped = row_swap(table, bit)
        table = jnp.where(far_row & bit != 0, swapped, table)
        bit *= 2

    group = [own_feat] + row_swaps([features] * n_row)[1:]
    cotangent = [own_cot] + chip_swaps([out_grad] * chips)[1:]
    cotangent += [col_swap(value, 1) for value in cotangent]

    work = 2 * half * total * width
    far = call(
        functools.partial(forward_body, 0),
        block(half),
        (dense, *group),
        (vmem,) * (1 + n_row),
        grant=grant,
        flops=work,
    )
    got_far = col_swap(far, 1)
    near = call(
        functools.partial(forward_body, half),
        block(half),
        (dense, *group),
        (vmem,) * (1 + n_row),
        grant=grant,
        flops=work,
    )
    sums = call(
        combine_body, [block(rows)] * chips, (near, got_far), (vmem,) * 2, moved=half * width * 6
    )
    sums = chip_swaps(sums)

    cot = call(
        functools.partial(pick_body, *sizes),
        [block(lanes)] * n_row,
        (table, *cotangent),
        (vmem,) * (1 + n_col),
        flops=4 * slots * rows * width,
    )
    cot = row_swaps(cot)

    grad, *sent = call(
        functools.partial(middle_body, n_row, chips),
        [block(rows)] + [block(lanes + marks + width)] * n_row,
        (slot, own_table, weight, *sums, *cot),
        (vmem,) * (3 + chips + n_row),
        flops=4 * slots * rows * width,
    )
    strip = chip_swaps([grad] * chips)
    other = [col_swap(value, 1) for value in strip]

    sent = row_swaps(sent)
    near_act, far_act = call(
        functools.partial(side_body, *sizes, all_marks),
        [block(slots // 2 + all_marks + width)] * 2,
        sent,
        (vmem,) * n_row,
        moved=slots * width * 4,
    )
    by_chip = call(
        functools.partial(chip_body, all_marks),
        [block(slots // chips + 2 * all_marks + width)] * chips,
        (near_act, col_swap(far_act, 1)),
        (vmem,) * 2,
        moved=slots * width * 4,
    )
    by_chip = chip_swaps(by_chip)

    part = call(
        functools.partial(backward_near_body, half),
        block(width, F32, total),
        (dense, *strip),
        (vmem,) * (1 + chips),
        grant=grant,
        flops=work,
    )
    part = call(
        functools.partial(backward_far_body, chips),
        [block(rows)] * n_row,
        (dense, part, *other),
        (vmem,) * (2 + chips),
        grant=grant,
        flops=work,
    )
    part = row_swaps(part)
    activations, weight_grad, feature_grad = call(
        functools.partial(final_body, n_row, span, all_marks, 1.0 / math.sqrt(rows * n_all)),
        [block(rows), block(width, F32), block(rows)],
        (weight, *part, *by_chip),
        (vmem,) * (1 + n_row + chips),
        flops=2 * (slots + width) * rows * width,
    )
    return (activations, feature_grad, weight_grad)


def solution(mesh):
    placed = (
        P(("row", "col"), None),
        P(),
        P("row", "col", None, None),
        P("row", "col"),
        P("row", "col"),
        P("row", "col"),
        P(("row", "col")),
        P(("row", "col"), None),
    )
    return jax.shard_map(
        layer,
        mesh=mesh,
        in_specs=placed,
        out_specs=(P(("row", "col"), None), P(("row", "col"), None), P()),
        check_vma=False,
    )
```

```python
import functools
import math

import jax
import jax.numpy as jnp
from jax import lax
from jax.experimental import pallas as pl
from jax.experimental.pallas import tpu as pltpu
from jax.sharding import PartitionSpec as P


BF16 = jnp.bfloat16
F32 = jnp.float32
I32 = jnp.int32
LANES = 128
GRANT = 16 << 20
KEPT = 24 << 20


def xor_pairs(size, bit):
    return [(i, i ^ bit) for i in range(size)]


def dot(a, b, left=1, right=0):
    return lax.dot_general(a, b, (((left,), (right,)), ((), ())), preferred_element_type=F32)


def iota(shape, dim):
    return lax.broadcasted_iota(I32, shape, dim)


def call(body, out_shape, operands, spaces, scratch=(), flops=0, moved=0, grant=GRANT):
    single = not isinstance(out_shape, (list, tuple))
    spec = pl.BlockSpec(memory_space=pltpu.VMEM)
    return pl.pallas_call(
        body,
        out_shape=out_shape,
        in_specs=[pl.BlockSpec(memory_space=space) for space in spaces],
        out_specs=spec if single else [spec] * len(out_shape),
        scratch_shapes=list(scratch),
        compiler_params=pltpu.CompilerParams(vmem_limit_bytes=grant),
        cost_estimate=pl.CostEstimate(flops=flops, bytes_accessed=moved, transcendentals=0),
    )(*operands)


def half_place(part, me, chips):
    far = part ^ me
    return (1 - (far & 1)) * chips + (far >> 1)


def build_body(
    sizes,
    dest_hbm,
    src_hbm,
    count_ref,
    source_hbm,
    feat_hbm,
    cot_hbm,
    tiles_ref,
    dense_ref,
    table_ref,
    other_ref,
    slot_ref,
    feat_ref,
    cot_ref,
    dest_ref,
    src_ref,
    source_ref,
    row_ref,
    col_ref,
    sem,
    near,
):
    n_row, n_col, span = sizes
    edge = tiles_ref.shape[-1]
    rows, cols = dense_ref.shape
    per = cols // (n_row * edge)
    chunk = 2 * edge
    my_row = lax.axis_index("row")
    my_col = lax.axis_index("col")
    loads = [
        pltpu.make_async_copy(dest_hbm, dest_ref, near.at[0]),
        pltpu.make_async_copy(src_hbm, src_ref, near.at[1]),
        pltpu.make_async_copy(source_hbm, source_ref, near.at[2]),
    ]
    rows_in = [
        pltpu.make_async_copy(feat_hbm, feat_ref, near.at[3]),
        pltpu.make_async_copy(cot_hbm, cot_ref, near.at[4]),
    ]
    for load in loads + rows_in:
        load.start()
    for part in range(n_col):
        for block in range(per):
            row_ref[part * per + block] = (half_place(part, my_col, n_col // 2) * per + block) * edge
    for part in range(n_row):
        for block in range(per):
            col_ref[part * per + block] = ((part ^ my_row) * per + block) * edge

    def clear(step, carry):
        at = pl.multiple_of(step * chunk, chunk)
        dense_ref[pl.ds(at, chunk), :] = jnp.zeros((chunk, cols), BF16)
        return carry

    lax.fori_loop(0, rows // chunk, clear, 0)
    for load in loads:
        load.wait()
    live = count_ref[0, 0]

    def start(slot):
        row = pl.multiple_of(row_ref[dest_ref[0, slot]], edge)
        col = pl.multiple_of(col_ref[src_ref[0, slot]], edge)
        pltpu.make_async_copy(
            tiles_ref.at[slot], dense_ref.at[pl.ds(row, edge), pl.ds(col, edge)], sem
        ).start()

    def start_some(step, carry):
        for at in range(4):
            start(step * 4 + at)
        return carry

    def start_one(slot, carry):
        start(slot)
        return carry

    some = live >> 2
    lax.fori_loop(0, some, start_some, 0)
    lax.fori_loop(some * 4, live, start_one, 0)

    slot_work(n_row, n_col, span, source_ref, table_ref, other_ref, slot_ref)
    for load in rows_in:
        load.wait()

    def arrived(count):
        part = dense_ref.at[pl.ds(0, edge), pl.ds(0, count * edge)]
        return pltpu.make_async_copy(part, part, sem)

    def wait_many(step, carry):
        arrived(8).wait()
        return carry

    def wait_one(step, carry):
        arrived(1).wait()
        return carry

    lax.fori_loop(0, live >> 3, wait_many, 0)
    lax.fori_loop(0, live & 7, wait_one, 0)


def slot_work(n_row, n_col, span, source_ref, table_ref, other_ref, slot_ref):
    rows = source_ref.shape[-1]
    slots = table_ref.shape[-1]
    n_all = n_row * n_col
    my_row = lax.axis_index("row")
    my_col = lax.axis_index("col")
    source = source_ref[...].reshape(1, rows)
    owner = ((source.astype(F32) + 0.5) * (1.0 / rows)).astype(I32)
    place = source - owner * rows + 1
    mine = iota((n_all, rows), 0) == owner
    before = (iota((rows, rows), 0) < iota((rows, rows), 1)).astype(BF16)
    earlier = dot(mine.astype(BF16), before)
    rank = jnp.sum(jnp.where(mine, earlier, 0.0), axis=0, keepdims=True).astype(I32)
    shift = n_col.bit_length() - 1
    far_row = (owner >> shift) ^ my_row
    far_col = (owner & (n_col - 1)) ^ my_col
    by_row = (far_row * n_col + far_col) * span + rank
    by_col = (far_col * n_row + far_row) * span + rank
    high = jnp.broadcast_to((place >> 7).astype(F32), (8, rows)).astype(BF16)
    low = jnp.broadcast_to((place & 127).astype(F32), (8, rows)).astype(BF16)
    for ref, order in ((table_ref, by_row), (other_ref, by_col)):
        hot = (iota((slots, rows), 0) == order).astype(BF16)
        ref[...] = (dot(high, hot, 1, 1) * 128.0 + dot(low, hot, 1, 1)).astype(I32)
    slot_ref[...] = jnp.broadcast_to(by_row, (8, rows))


def pick_body(n_row, n_col, span, table_ref, *refs):
    cot = refs[:n_col]
    out = refs[n_col:]
    rows = cot[0].shape[0]
    tail = n_row * span
    for base in range(0, n_col * tail, LANES):
        place = table_ref[0:1, base : base + LANES]
        hot = (iota((rows, LANES), 0) + 1 == place).astype(BF16)
        for k in range(base // tail, -(-(base + LANES) // tail)):
            picked = dot(hot, cot[(k >> 1) + (k & 1) * (n_col // 2)][...], 0, 0).astype(BF16)
            for r in range(n_row):
                at = k * tail + r * span - base
                if 0 <= at < LANES:
                    out[r][k * span : (k + 1) * span, :] = picked[at : at + span, :]


def tree_sum(terms):
    terms = [term.astype(F32) for term in terms]
    while len(terms) > 1:
        terms = [terms[at] + terms[at + 1] for at in range(0, len(terms), 2)]
    return terms[0]


def forward_body(first, dense_ref, *refs):
    out = refs[-1]
    feat = jnp.concatenate([ref[...] for ref in refs[:-1]], axis=0)
    count = out.shape[0]
    step = 512 if count % 512 == 0 else 128
    for at in range(0, count, step):
        out[at : at + step, :] = dot(dense_ref[first + at : first + at + step, :], feat).astype(BF16)


def combine_body(own_ref, got_ref, *out):
    rows = out[0].shape[0]
    for at, ref in enumerate(out):
        part = slice(at * rows, (at + 1) * rows)
        ref[...] = (own_ref[part, :].astype(F32) + got_ref[part, :].astype(F32)).astype(BF16)


def middle_body(n_row, chips, slot_ref, table_ref, weight_ref, *refs):
    got = refs[:chips]
    back = refs[chips : chips + n_row]
    grad_ref = refs[chips + n_row]
    out = refs[chips + n_row + 1 :]
    rows, width = grad_ref.shape
    slots = table_ref.shape[1]
    lanes = slots // n_row
    marks = out[0].shape[0] - lanes - width
    mixed = got[0][...].astype(F32)
    for ref in got[1:]:
        mixed = mixed + ref[...].astype(F32)
    mixed = mixed.astype(BF16)
    pre = dot(mixed, weight_ref[...]).astype(BF16).astype(F32)
    sigma = jax.nn.sigmoid(pre)
    act = (pre * sigma).astype(BF16)
    returned = jnp.concatenate([ref[...] for ref in back], axis=0)
    hot = (iota((slots, rows), 0) == slot_ref[0:1, :]).astype(BF16)
    dest_grad = dot(hot, returned, 0, 0)
    grad = (dest_grad * (sigma * (1.0 + pre * (1.0 - sigma)))).astype(BF16)
    grad_ref[...] = grad
    sent = dot(hot, act).astype(BF16)
    term = dot(mixed, grad, 0, 0).astype(BF16)
    row = iota((marks, LANES), 0)
    for r in range(n_row):
        out[r][:lanes, :] = sent[r * lanes : (r + 1) * lanes, :]
        block = jnp.zeros((marks, LANES), F32)
        for piece in range(lanes // LANES):
            at = r * lanes + piece * LANES
            place = table_ref[0:1, at : at + LANES]
            block = jnp.where(row == 2 * piece, (place >> 7).astype(F32), block)
            block = jnp.where(row == 2 * piece + 1, (place & 127).astype(F32), block)
        out[r][lanes : lanes + marks, :] = block.astype(BF16)
        out[r][lanes + marks :, :] = term


def side_body(n_row, n_col, span, all_marks, *refs):
    got = refs[:n_row]
    sides = refs[n_row:]
    lanes = n_col * span
    width = got[0].shape[1]
    marks = got[0].shape[0] - lanes - width
    base = lanes * n_row // 2
    lines = 2 * (lanes // LANES)
    row = iota((all_marks, LANES), 0)
    block = jnp.zeros((all_marks, LANES), F32)
    for r in range(n_row):
        for k in range(n_col):
            at = ((k >> 1) * n_row + r) * span
            sides[k & 1][at : at + span, :] = got[r][k * span : (k + 1) * span, :]
        held = got[r][lanes : lanes + marks, :].astype(F32)
        for line in range(lines):
            block = jnp.where(row == r * lines + line, held[line : line + 1, :], block)
    term = tree_sum([ref[lanes + marks :, :] for ref in got]).astype(BF16)
    for ref in sides:
        ref[base : base + all_marks, :] = block.astype(BF16)
        ref[base + all_marks :, :] = term


def chip_body(marks, near_ref, far_ref, *out):
    width = near_ref.shape[1]
    base = near_ref.shape[0] - marks - width
    size = base // len(out)
    term = (near_ref[base + marks :, :].astype(F32) + far_ref[base + marks :, :].astype(F32)).astype(BF16)
    for q, ref in enumerate(out):
        for side, src in enumerate((near_ref, far_ref)):
            ref[side * size : (side + 1) * size, :] = src[q * size : (q + 1) * size, :]
            at = 2 * size + side * marks
            ref[at : at + marks, :] = src[base : base + marks, :]
        ref[2 * size + 2 * marks :, :] = term


def product(dense_ref, first, grads, at, size):
    grad = jnp.concatenate([ref[...].T for ref in grads], axis=1)
    return dot(grad, dense_ref[first : first + grad.shape[1], at : at + size])


def backward_near_body(first, dense_ref, *refs):
    out = refs[-1]
    width = 2 * LANES
    for at in range(0, out.shape[1], width):
        size = min(width, out.shape[1] - at)
        out[:, at : at + size] = product(dense_ref, first, refs[:-1], at, size)


def backward_far_body(chips, first, dense_ref, near_ref, *refs):
    grads = refs[:chips]
    out = refs[chips:]
    rows = out[0].shape[0]
    width = 2 * LANES
    stop = first + len(out) * rows
    for at in range(first, stop, width):
        size = min(width, stop - at)
        part = product(dense_ref, 0, grads, at, size) + near_ref[:, at : at + size]
        part = part.T.astype(BF16)
        for half in range(0, size, LANES):
            r, row = divmod(at + half - first, rows)
            out[r][row : row + LANES, :] = part[half : half + LANES, :]


def final_body(n_row, span, all_marks, scale, weight_ref, *refs):
    act_ref, total_ref, grad_ref = refs[-3:]
    parts = refs[:n_row]
    got = refs[n_row:-3]
    chips = len(got)
    rows, width = act_ref.shape
    lanes = 2 * chips * span
    size = n_row * span
    total_ref[...] = tree_sum([ref[2 * size + 2 * all_marks :, :] for ref in got]) * scale
    act = jnp.zeros((rows, width), F32)
    lane = iota((1, LANES), 1)
    for r in range(n_row):
        held = []
        for q in range(chips):
            for side in range(2):
                at = side * size + r * span
                held.append(got[q][at : at + span, :])
        held = jnp.concatenate(held, axis=0)
        for piece in range(lanes // LANES):
            place = jnp.zeros((1, LANES), F32)
            for k in range(2 * chips):
                at = k * span - piece * LANES
                if 0 <= at < LANES:
                    base = 2 * size + (k & 1) * all_marks + 2 * (r * (lanes // LANES) + piece)
                    pair = got[k >> 1][base - base % 8 : base - base % 8 + 8, :].astype(F32)
                    high = pair[base % 8 : base % 8 + 1, :]
                    low = pair[base % 8 + 1 : base % 8 + 2, :]
                    inside = (lane >= at) & (lane < at + span)
                    place = jnp.where(inside, high * 128.0 + low, place)
            hot = (iota((rows, LANES), 0) + 1 == place.astype(I32)).astype(BF16)
            act = act + dot(hot, held[piece * LANES : (piece + 1) * LANES, :])
    act_ref[...] = act.astype(BF16)
    hidden = tree_sum([ref[...] for ref in parts])
    grad_ref[...] = dot(hidden.astype(BF16), weight_ref[...], 1, 1).astype(BF16)


def layer(features, weight, tiles, tile_dest, tile_src, tile_count, source_of, out_grad):
    rows, width = features.shape
    edge = tiles.shape[-1]
    n_row = lax.axis_size("row")
    n_col = lax.axis_size("col")
    n_all = n_row * n_col
    chips = n_col // 2
    span = -(-(rows // n_all) // 16) * 16
    slots = n_all * span
    lanes = n_col * span
    marks = -(-2 * (lanes // LANES) // 16) * 16
    all_marks = -(-2 * (slots // LANES) // 16) * 16
    sizes = (n_row, n_col, span)
    total = n_row * rows
    half = chips * rows
    vmem = pltpu.VMEM

    def row_swap(value, bit):
        return lax.ppermute(value, "row", xor_pairs(n_row, bit))

    def col_swap(value, bit):
        return lax.ppermute(value, "col", xor_pairs(n_col, bit))

    def row_swaps(values):
        return [values[0]] + [row_swap(values[k], k) for k in range(1, n_row)]

    def chip_swaps(values):
        return [values[0]] + [col_swap(values[k], 2 * k) for k in range(1, chips)]

    def block(count, kind=BF16, across=width):
        return jax.ShapeDtypeStruct((count, across), kind)

    dense_bytes = 4 * half * total
    kept = dense_bytes <= KEPT
    grant = GRANT if kept else dense_bytes + GRANT
    hbm = pltpu.HBM
    far_memory = lambda value: pltpu.with_memory_space_constraint(value, hbm)
    dense, own_table, table, slot, own_feat, own_cot = call(
        functools.partial(build_body, sizes),
        [
            pltpu.VMEM((2 * half, total), BF16) if kept else block(2 * half, BF16, total),
            block(8, I32, slots),
            block(8, I32, slots),
            block(8, I32, rows),
            block(rows),
            block(rows),
        ],
        (
            far_memory(tile_dest),
            far_memory(tile_src),
            tile_count,
            far_memory(source_of),
            far_memory(features),
            far_memory(out_grad),
            far_memory(tiles.reshape(tiles.shape[1:])),
        ),
        (hbm, hbm, pltpu.SMEM, hbm, hbm, hbm, hbm),
        scratch=[
            pltpu.SMEM(tile_dest.shape, I32),
            pltpu.SMEM(tile_src.shape, I32),
            pltpu.VMEM(source_of.shape, I32),
            pltpu.SMEM((2 * half // edge,), I32),
            pltpu.SMEM((total // edge,), I32),
            pltpu.SemaphoreType.DMA,
            pltpu.SemaphoreType.DMA((5,)),
        ],
        grant=grant,
        moved=tiles.size * 2,
    )
    far_row = jnp.arange(slots)[None, :] // span % n_row
    bit = 1
    while bit < n_row:
        swapped = row_swap(table, bit)
        table = jnp.where(far_row & bit != 0, swapped, table)
        bit *= 2

    group = [own_feat] + row_swaps([features] * n_row)[1:]
    cotangent = [own_cot] + chip_swaps([out_grad] * chips)[1:]
    cotangent += [col_swap(value, 1) for value in cotangent]

    work = 2 * half * total * width
    far = call(
        functools.partial(forward_body, 0),
        block(half),
        (dense, *group),
        (vmem,) * (1 + n_row),
        grant=grant,
        flops=work,
    )
    got_far = col_swap(far, 1)
    near = call(
        functools.partial(forward_body, half),
        block(half),
        (dense, *group),
        (vmem,) * (1 + n_row),
        grant=grant,
        flops=work,
    )
    sums = call(
        combine_body, [block(rows)] * chips, (near, got_far), (vmem,) * 2, moved=half * width * 6
    )
    sums = chip_swaps(sums)

    cot = call(
        functools.partial(pick_body, *sizes),
        [block(lanes)] * n_row,
        (table, *cotangent),
        (vmem,) * (1 + n_col),
        flops=4 * slots * rows * width,
    )
    cot = row_swaps(cot)

    grad, *sent = call(
        functools.partial(middle_body, n_row, chips),
        [block(rows)] + [block(lanes + marks + width)] * n_row,
        (slot, own_table, weight, *sums, *cot),
        (vmem,) * (3 + chips + n_row),
        flops=4 * slots * rows * width,
    )
    strip = chip_swaps([grad] * chips)
    other = [col_swap(value, 1) for value in strip]

    sent = row_swaps(sent)
    near_act, far_act = call(
        functools.partial(side_body, *sizes, all_marks),
        [block(slots // 2 + all_marks + width)] * 2,
        sent,
        (vmem,) * n_row,
        moved=slots * width * 4,
    )
    by_chip = call(
        functools.partial(chip_body, all_marks),
        [block(slots // chips + 2 * all_marks + width)] * chips,
        (near_act, col_swap(far_act, 1)),
        (vmem,) * 2,
        moved=slots * width * 4,
    )
    by_chip = chip_swaps(by_chip)

    part = call(
        functools.partial(backward_near_body, half),
        block(width, F32, total),
        (dense, *strip),
        (vmem,) * (1 + chips),
        grant=grant,
        flops=work,
    )
    near_part = part
    part = []
    for first in (n_row // 2, 0):
        blocks = call(
            functools.partial(backward_far_body, chips, first * rows),
            [block(rows)] * (n_row // 2),
            (dense, near_part, *other),
            (vmem,) * (2 + chips),
            grant=grant,
            flops=work // 2,
        )
        part = [*blocks, *part]
    part = row_swaps(part)
    activations, weight_grad, feature_grad = call(
        functools.partial(final_body, n_row, span, all_marks, 1.0 / math.sqrt(rows * n_all)),
        [block(rows), block(width, F32), block(rows)],
        (weight, *part, *by_chip),
        (vmem,) * (1 + n_row + chips),
        flops=2 * (slots + width) * rows * width,
    )
    return (activations, feature_grad, weight_grad)


def solution(mesh):
    placed = (
        P(("row", "col"), None),
        P(),
        P("row", "col", None, None),
        P("row", "col"),
        P("row", "col"),
        P("row", "col"),
        P(("row", "col")),
        P(("row", "col"), None),
    )
    return jax.shard_map(
        layer,
        mesh=mesh,
        in_specs=placed,
        out_specs=(P(("row", "col"), None), P(("row", "col"), None), P()),
        check_vma=False,
    )
```
